256 devices in a mesh: seq: 64 (over y, z_hi, x), head: 4 (over z_lo, core).
Axes of the slice: x: 4, y: 4, z: 8 (z_hi: 4, z_lo: 2; z = z_hi * 2 + z_lo), core: 2. Of those that a mesh axis runs over, the one named last changes fastest.
Arguments:
- inputs: bfloat16 [256, 512, 768], P('seq'), may hold values from -6 to 6
- out_grad: bfloat16 [256, 512, 768], P('seq'), may hold values from -16 to 16
- w_query: bfloat16 [768, 512], P(None, 'head'), may hold values from -0.21875 to 0.21875
- w_key: bfloat16 [768, 512], P(None, 'head'), may hold values from -0.21875 to 0.21875
- w_value: bfloat16 [768, 512], P(None, 'head'), may hold values from -0.21875 to 0.21875
- w_output: bfloat16 [512, 768], P('head'), may hold values from -0.25 to 0.25
Outputs:
- grad_inputs: bfloat16 [256, 512, 768], P('seq', 'head')
- grad_wq: float32 [768, 512], P(None, 'head')
- grad_wk: float32 [768, 512], P(None, 'head')
- grad_wv: float32 [768, 512], P(None, 'head')
- grad_wo: float32 [512, 768], P('head')
The draws below stay inside these ranges and needn't reach their ends.
All inputs are finite; a program needn't handle non-finite values.
Results may differ from the reference program's by a relative error of at most 0.012.
Values may be sent and summed in bfloat16 or wider, within the bound.
A program may use at most 64 MiB of HBM per device.

```python
import math
import jax
import jax.numpy as jnp
from jax import lax

D = 768
HEAD_DIM = 64
HEADS = 8
COLS = 512
ROWS = 256
TOKENS = 131072
HD = 512


def block_levels(own_key, extent, shards, low, high):
    gain = 1.0
    for dim, parts in shards:
        draws = jax.random.uniform(jax.random.fold_in(jax.random.fold_in(own_key, 6), dim), (parts,), jnp.float32, low / len(shards), high / len(shards))
        gain = gain * jnp.repeat(jnp.exp(draws), extent[dim] // parts).reshape((-1,) + (1,) * (len(extent) - 1 - dim))
    return gain


def bell_draw(key, extent, deviation, most, shards=(), held_as=jnp.bfloat16):
    array = jax.random.normal(key, extent, jnp.float32) * deviation
    if len(shards) > 0:
        array = block_levels(key, extent, shards, -0.22, 0.18) * array
    return jnp.clip(array, min=-most, max=most).astype(held_as)


def setup_inputs(seed: int = 0) -> dict:
    keys = jax.random.split(jax.random.key(seed), 7)
    inputs = bell_draw(keys[0], (ROWS, COLS, D), 1.0, 6.0, ((0, 64),))
    out_grad = bell_draw(keys[1], (ROWS, COLS, D), 4.0, 16.0, ((0, 64),))
    w_query = bell_draw(keys[2], (D, HD), D ** -0.5, 0.21875, ((1, 4),))
    w_key = bell_draw(keys[3], (D, HD), D ** -0.5, 0.21875, ((1, 4),))
    w_value = bell_draw(keys[4], (D, HD), D ** -0.5, 0.21875, ((1, 4),))
    w_output = bell_draw(keys[5], (HD, D), HD ** -0.5, 0.25, ((0, 4),))
    return {"inputs": inputs, "out_grad": out_grad, "w_query": w_query, "w_key": w_key, "w_value": w_value, "w_output": w_output}


def projected(source, matrix):
    flat = source.reshape(-1, source.shape[-1])
    return jnp.dot(flat, matrix, preferred_element_type=jnp.float32).astype(jnp.bfloat16)

def reference(inputs, out_grad, w_query, w_key, w_value, w_output):
    row_count, col_count, model_width = inputs.shape
    logit_scale = 1.0 / (math.sqrt(HEAD_DIM) * math.sqrt(ROWS))
    inv_root = 1.0 / math.sqrt(TOKENS)
    shape_heads = (row_count, col_count, HEADS, HEAD_DIM)
    query_proj = projected(inputs, w_query)
    key_proj = projected(inputs, w_key)
    value_proj = projected(inputs, w_value)
    query_four = query_proj.reshape(shape_heads).astype(jnp.float32)
    key_four = key_proj.reshape(shape_heads).astype(jnp.float32)
    value_four = value_proj.reshape(shape_heads).astype(jnp.float32)
    logits = logit_scale * jnp.einsum('rihe,rjhe->hij', query_four, key_four)
    exponent = jnp.exp(logits)
    attn_probs = exponent / lax.optimization_barrier(jnp.sum(exponent, axis=2, keepdims=True))
    probs_low = attn_probs.astype(jnp.bfloat16)
    attended = jnp.einsum('hij,rjhe->rihe', probs_low.astype(jnp.float32), value_four).astype(jnp.bfloat16)
    flat_in = inputs.reshape(-1, model_width)
    flat_grad = out_grad.reshape(-1, model_width)
    grad_wo = jnp.dot(attended.reshape(-1, HD).T, flat_grad, preferred_element_type=jnp.float32) * inv_root
    grad_att = jnp.dot(flat_grad, w_output.T, preferred_element_type=jnp.float32).astype(jnp.bfloat16)
    grad_four = grad_att.reshape(shape_heads).astype(jnp.float32)
    grad_probs = jnp.einsum('rihe,rjhe->hij', grad_four, value_four)
    row_inner = lax.optimization_barrier(jnp.sum(attn_probs * grad_probs, axis=2, keepdims=True))
    grad_logits = (logit_scale * attn_probs * (grad_probs - row_inner)).astype(jnp.bfloat16)
    logit_four = grad_logits.astype(jnp.float32)
    grad_value = jnp.einsum('hij,rihe->rjhe', probs_low.astype(jnp.float32), grad_four).astype(jnp.bfloat16)
    grad_query = jnp.einsum('hij,rjhe->rihe', logit_four, key_four).astype(jnp.bfloat16)
    grad_key = jnp.einsum('hij,rihe->rjhe', logit_four, query_four).astype(jnp.bfloat16)
    flat_q = grad_query.reshape(-1, HD)
    flat_k = grad_key.reshape(-1, HD)
    flat_v = grad_value.reshape(-1, HD)
    grad_flat = jnp.dot(flat_q, w_query.T, preferred_element_type=jnp.float32)
    grad_flat = grad_flat + jnp.dot(flat_k, w_key.T, preferred_element_type=jnp.float32)
    grad_flat = grad_flat + jnp.dot(flat_v, w_value.T, preferred_element_type=jnp.float32)
    grad_inputs = grad_flat.astype(jnp.bfloat16).reshape(row_count, col_count, model_width)
    grad_wq = jnp.dot(flat_in.T, flat_q, preferred_element_type=jnp.float32) * inv_root
    grad_wk = jnp.dot(flat_in.T, flat_k, preferred_element_type=jnp.float32) * inv_root
    grad_wv = jnp.dot(flat_in.T, flat_v, preferred_element_type=jnp.float32) * inv_root
    return (grad_inputs, grad_wq, grad_wk, grad_wv, grad_wo)
```

```python
import math

import jax
import jax.numpy as jnp
from jax import lax
from jax.experimental import pallas as pl
from jax.experimental.pallas import tpu as pltpu
from jax.sharding import Mesh
from jax.sharding import PartitionSpec as P

AXES = ("y", "zh", "x", "zl", "core")
SEQ = ("y", "zh", "x")
HEAD = ("zl", "core")
ROWS, COLS, D, HEAD_DIM, HEADS = 4, 512, 768, 64, 2
WIDTH = HEADS * HEAD_DIM
ALL_ROWS = 256
C = 1.0 / (math.sqrt(HEAD_DIM) * math.sqrt(ALL_ROWS))
INV_ROOT = 1.0 / math.sqrt(ALL_ROWS * COLS)
COPIES = 128
F32, BF16 = jnp.float32, jnp.bfloat16


def nt(a, b):
    return lax.dot_general(a, b, (((1,), (1,)), ((), ())), preferred_element_type=F32)


def nn(a, b):
    return lax.dot_general(a, b, (((1,), (0,)), ((), ())), preferred_element_type=F32)


def tn(a, b):
    return lax.dot_general(a, b, (((0,), (0,)), ((), ())), preferred_element_type=F32)


class Copies:
    def __init__(self, send_sem, recv_sem):
        self.send_sem, self.recv_sem, self.made = send_sem, recv_sem, []

    def send(self, src, dst, device):
        k = len(self.made)
        copy = pltpu.make_async_remote_copy(
            src_ref=src,
            dst_ref=dst,
            send_sem=self.send_sem.at[k],
            recv_sem=self.recv_sem.at[k],
            device_id=device,
            device_id_type=pl.DeviceIdType.MESH,
        )
        copy.start()
        self.made.append(copy)
        return copy

    def drain(self):
        for copy in self.made:
            copy.wait_send()


class RingSum:
    def __init__(self, copies, piece, rel, rcv, tmp, right, left):
        self.copies, self.piece, self.rel, self.rcv, self.tmp = copies, piece, rel, rcv, tmp
        self.right, self.left = right, left

    def start(self):
        send, piece = self.copies.send, self.piece
        self.c1 = send(piece(2, 0), self.rel.at[0], self.right)
        self.c2 = send(piece(2, 1), self.rel.at[1], self.left)
        self.c3 = send(piece(1, 1), self.rcv.at[0, 1], self.right)
        self.c4 = send(piece(3, 0), self.rcv.at[1, 0], self.left)

    def relay(self):
        send, piece = self.copies.send, self.piece
        self.c1.wait_recv()
        self.tmp[0] = (piece(1, 0)[...].astype(F32) + self.rel[0].astype(F32)).astype(BF16)
        self.c2.wait_recv()
        self.tmp[1] = (piece(3, 1)[...].astype(F32) + self.rel[1].astype(F32)).astype(BF16)
        self.c5 = send(self.tmp.at[0], self.rcv.at[0, 0], self.right)
        self.c6 = send(self.tmp.at[1], self.rcv.at[1, 1], self.left)

    def finish(self):
        for copy in (self.c3, self.c4, self.c5, self.c6):
            copy.wait_recv()
        return [
            self.piece(0, half)[...].astype(F32)
            + self.rcv[0, half].astype(F32)
            + self.rcv[1, half].astype(F32)
            for half in range(2)
        ]


class RingGather:
    def __init__(self, copies, block, right, left):
        self.copies, self.block, self.right, self.left = copies, block, right, left

    def start(self):
        whole = self.block(0, None)
        self.d1 = self.copies.send(whole, whole, self.right)
        self.d2 = self.copies.send(whole, whole, self.left)

    def relay(self):
        self.d1.wait_recv()
        far = self.block(3, 0)
        self.e1 = self.copies.send(far, far, self.right)
        self.d2.wait_recv()
        far = self.block(1, 1)
        self.e2 = self.copies.send(far, far, self.left)

    def finish(self):
        self.e1.wait_recv()
        self.e2.wait_recv()


def kernel(
    x_hbm, g_hbm, wq_hbm, wk_hbm, wv_hbm, wo_hbm,
    gin_ref, wt_ref,
    xv, gv, wo, wfull, wt, proj, part,
    rel1, rcv1, tmp1, sum1, rel2, rcv2, tmp2, sum2, rcv3,
    pd, att, grad, gall,
    wacc, wpart, wrel1, wrcv1, wtmp1, wsum1, wrel2, wrcv2, wtmp2, wrcv3, wfin,
    load_sem, send_sem, recv_sem,
):
    y, zh, x, zl, co = (lax.axis_index(n) for n in AXES)
    a = x * (1 - co) + y * co
    b = y * (1 - co) + x * co
    head = zl * 2 + co

    def dev(da=0, db=0, dc=0, dzl=0, dco=0):
        return (
            lax.rem(y + da * co + db * (1 - co), 4),
            lax.rem(zh + dc, 4),
            lax.rem(x + da * (1 - co) + db * co, 4),
            lax.rem(zl + dzl, 2),
            lax.rem(co + dco, 2),
        )

    a_right, a_left = dev(da=1), dev(da=3)
    b_right, b_left = dev(db=1), dev(db=3)
    z_others = [dev(dc=k) for k in (1, 2, 3)]
    h_core, h_chip, h_both = dev(dco=1), dev(dzl=1), dev(dzl=1, dco=1)

    def at_a(off, size):
        return pl.ds(pl.multiple_of(lax.rem(a + off, 4) * size, size), size)

    mine = pl.ds(pl.multiple_of(head * WIDTH, WIDTH), WIDTH)
    loads = [
        pltpu.make_async_copy(w.at[...], wfull.at[t, :, mine], load_sem.at[t])
        for t, w in enumerate((wq_hbm, wk_hbm, wv_hbm))
    ]
    loads.append(pltpu.make_async_copy(x_hbm, xv, load_sem.at[3]))
    loads.append(pltpu.make_async_copy(wo_hbm, wo, load_sem.at[4]))
    loads.append(pltpu.make_async_copy(g_hbm, gv, load_sem.at[5]))
    for load in loads:
        load.start()

    barrier = pltpu.get_barrier_semaphore()
    friends = [a_right, a_left, b_right, b_left, *z_others, h_core, h_chip, h_both]
    for friend in friends:
        pl.semaphore_signal(barrier, inc=1, device_id=friend, device_id_type=pl.DeviceIdType.MESH)

    copies = Copies(send_sem, recv_sem)
    for load in loads[:4]:
        load.wait()
    for t in range(3):
        wt[t * WIDTH : (t + 1) * WIDTH, :] = wfull[t, :, mine].T

    def project(r, _):
        res = nt(wt[...], xv[r]).astype(BF16)
        at = pl.ds(pl.multiple_of(r * HEAD_DIM, HEAD_DIM), HEAD_DIM)
        for t in range(3):
            for h in range(HEADS):
                k = t * WIDTH + h * HEAD_DIM
                proj[t, h, at, :] = res[k : k + HEAD_DIM]
        return 0

    lax.fori_loop(0, ROWS, project, 0)

    def products(m, left, right):
        def one(k, _):
            h, blk = k // 4, lax.rem(k, 4)
            at = pl.ds(pl.multiple_of(blk * 128, 128), 128)
            part[m, h, at, :] = tn(proj[left, h, :, at], proj[right, h]).astype(BF16)
            return 0

        lax.fori_loop(0, 4 * HEADS, one, 0)

    products(0, 0, 1)
    pl.semaphore_wait(barrier, len(friends))

    def ring1(m):
        return RingSum(
            copies,
            lambda off, half: part.at[m, half, at_a(off, 128), :],
            rel1.at[m], rcv1.at[m], tmp1.at[m], a_right, a_left,
        )

    first = [ring1(0), ring1(1)]
    first[0].start()
    to_core = [copies.send(wfull.at[t, :, mine], wfull.at[t, :, mine], h_core) for t in range(3)]
    to_chip = [copies.send(wfull.at[t, :, mine], wfull.at[t, :, mine], h_chip) for t in range(3)]

    for load in loads[4:]:
        load.wait()

    def project_grad(r, _):
        res = nt(wo[...], gv[r]).astype(BF16)
        at = pl.ds(pl.multiple_of(r * HEAD_DIM, HEAD_DIM), HEAD_DIM)
        for h in range(HEADS):
            proj[3, h, at, :] = res[h * HEAD_DIM : (h + 1) * HEAD_DIM]
        return 0

    lax.fori_loop(0, ROWS, project_grad, 0)
    products(1, 3, 2)
    first[1].start()

    def at_b(off, size):
        return pl.ds(pl.multiple_of(lax.rem(b + off, 4) * size, size), size)

    def ring2(m):
        return RingSum(
            copies,
            lambda off, half: sum1.at[m, half, at_b(off, 32), :],
            rel2.at[m], rcv2.at[m], tmp2.at[m], b_right, b_left,
        )

    second = [ring2(0), ring2(1)]
    first[0].relay()
    first[1].relay()
    for m in range(2):
        for half, total in enumerate(first[m].finish()):
            sum1[m, half] = total.astype(BF16)
        second[m].start()
    second[0].relay()
    second[1].relay()

    other = lax.rem(zl + 1, 2) * 2 + co
    theirs = pl.ds(pl.multiple_of(other * WIDTH, WIDTH), WIDTH)
    forward = []
    for t in range(3):
        to_chip[t].wait_recv()
        forward.append(copies.send(wfull.at[t, :, theirs], wfull.at[t, :, theirs], h_core))

    def spot(off):
        place = lax.rem(zh + off, 4)
        return place // 2, pl.ds(pl.multiple_of(lax.rem(place, 2) * 16, 16), 16)

    third = []
    for m in range(2):
        for half, total in enumerate(second[m].finish()):
            sum2[m, half] = total.astype(BF16)
        third.append([])
        for k in range(3):
            h, at = spot(k + 1)
            third[m].append(copies.send(sum2.at[m, h, at, :], rcv3.at[m, k], z_others[k]))

    totals = []
    for m in range(2):
        h, at = spot(0)
        total = sum2[m, h, at, :].astype(F32)
        for k in range(3):
            third[m][k].wait_recv()
            total = total + rcv3[m, k].astype(F32)
        totals.append(total)

    exponent = jnp.exp(C * totals[0])
    probs = exponent / jnp.sum(exponent, axis=1, keepdims=True)
    inner = jnp.sum(probs * totals[1], axis=1, keepdims=True)
    dlog = C * probs * (totals[1] - inner)
    own_h, _ = spot(0)
    row = a * 128 + b * 32 + lax.rem(zh, 2) * 16
    own_rows = pl.ds(pl.multiple_of(row, 16), 16)
    pd[0, own_h, own_rows, :] = probs.astype(BF16)
    pd[1, own_h, own_rows, :] = dlog.astype(BF16)
    own = pd.at[:, own_h, own_rows, :]
    spread = [copies.send(own, own, z_others[k]) for k in range(3)]
    for copy in spread:
        copy.wait_recv()

    def block_b(off, half):
        row = a * 128 + lax.rem(b + off, 4) * 32
        at = pl.ds(pl.multiple_of(row, 32), 32)
        return pd.at[:, :, at, :] if half is None else pd.at[:, half, at, :]

    gather_b = RingGather(copies, block_b, b_right, b_left)
    gather_b.start()
    gather_b.relay()
    gather_b.finish()

    def block_a(m):
        def block(off, half):
            at = at_a(off, 128)
            return pd.at[m, :, at, :] if half is None else pd.at[m, half, at, :]

        return block

    gather_a = [RingGather(copies, block_a(m), a_right, a_left) for m in range(2)]
    gather_a[0].start()
    gather_a[1].start()
    gather_a[0].relay()
    gather_a[0].finish()

    def pair_value(h, _):
        p = pd[0, h]
        att[h] = nt(proj[2, h], p).astype(BF16).reshape(ROWS, HEAD_DIM, COLS)
        grad[2, h] = nn(proj[3, h], p).astype(BF16).reshape(ROWS, HEAD_DIM, COLS)
        return 0

    lax.fori_loop(0, HEADS, pair_value, 0)
    gather_a[1].relay()

    def to_heads(t):
        sent = []
        for device, dzl, dco in ((h_chip, 1, 0), (h_both, 1, 1), (h_core, 0, 1)):
            h = lax.rem(zl + dzl, 2) * 2 + lax.rem(co + dco, 2)
            at = pl.ds(pl.multiple_of(h * 128, 128), 128)
            sent.append(copies.send(grad.at[t, :, :, :, at], gall.at[t, head], device))
        keep = pltpu.make_async_copy(grad.at[t, :, :, :, mine], gall.at[t, head], load_sem.at[6 + t])
        keep.start()
        return sent, keep

    moved = {2: to_heads(2)}

    def weight_part(p, kinds):
        def one(r, _):
            for k, (source, t) in enumerate(kinds):
                src = att if t is None else grad.at[t]
                lhs = jnp.concatenate([src[0, r], src[1, r]], axis=0)
                at = slice(k * WIDTH, (k + 1) * WIDTH)
                wacc[at, :] = jnp.where(r == 0, 0.0, wacc[at, :]) + nn(lhs, source[r])
            return 0

        lax.fori_loop(0, ROWS, one, 0)
        wpart[p] = wacc[...].astype(BF16)

    def halves(half):
        return slice(half * 384, (half + 1) * 384)

    def wring1(p):
        return RingSum(
            copies,
            lambda off, half: wpart.at[p, at_a(off, 64), halves(half)],
            wrel1.at[p], wrcv1.at[p], wtmp1.at[p], a_right, a_left,
        )

    def wring2(p):
        return RingSum(
            copies,
            lambda off, half: wsum1.at[p, at_b(off, 16), halves(half)],
            wrel2.at[p], wrcv2.at[p], wtmp2.at[p], b_right, b_left,
        )

    wfirst = [wring1(0), wring1(1)]
    wsecond = [wring2(0), wring2(1)]
    weight_part(0, ((xv, 2), (gv, None)))
    wfirst[0].start()
    gather_a[1].finish()

    def pair_score(h, _):
        d = pd[1, h]
        grad[0, h] = nt(proj[1, h], d).astype(BF16).reshape(ROWS, HEAD_DIM, COLS)
        grad[1, h] = nn(proj[0, h], d).astype(BF16).reshape(ROWS, HEAD_DIM, COLS)
        return 0

    lax.fori_loop(0, HEADS, pair_score, 0)
    moved[0] = to_heads(0)
    moved[1] = to_heads(1)
    wfirst[0].relay()
    weight_part(1, ((xv, 0), (xv, 1)))
    wfirst[1].start()

    def end_first(p):
        for half, total in enumerate(wfirst[p].finish()):
            wsum1[p, :, halves(half)] = total.astype(BF16)
        wsecond[p].start()

    wthird = []

    def end_second(p):
        for half, total in enumerate(wsecond[p].finish()):
            wrcv3[p, zh, :, halves(half)] = total.astype(BF16)
        own = wrcv3.at[p, zh]
        wthird.append([copies.send(own, own, device) for device in z_others])

    wgather_b, wgather_a = [], []

    def end_third(p):
        for copy in wthird[p]:
            copy.wait_recv()
        total = wrcv3[p, 0].astype(F32) + wrcv3[p, 1].astype(F32)
        total = total + wrcv3[p, 2].astype(F32) + wrcv3[p, 3].astype(F32)
        wfin[p, pl.ds(pl.multiple_of(a * 64 + b * 16, 16), 16), :] = total.astype(BF16)

        def block_b(off, half):
            at = pl.ds(pl.multiple_of(a * 64 + lax.rem(b + off, 4) * 16, 16), 16)
            return wfin.at[p, at, :] if half is None else wfin.at[p, at, halves(half)]

        def block_a(off, half):
            at = at_a(off, 64)
            return wfin.at[p, at, :] if half is None else wfin.at[p, at, halves(half)]

        wgather_b.append(RingGather(copies, block_b, b_right, b_left))
        wgather_a.append(RingGather(copies, block_a, a_right, a_left))
        wgather_b[p].start()

    end_first(0)
    wsecond[0].relay()
    wfirst[1].relay()
    end_second(0)
    end_first(1)
    wsecond[1].relay()
    end_third(0)
    end_second(1)
    wgather_b[0].relay()
    wgather_b[0].finish()
    wgather_a[0].start()
    end_third(1)
    wgather_a[0].relay()
    wgather_b[1].relay()
    wgather_b[1].finish()
    wgather_a[1].start()
    wgather_a[1].relay()

    for copy in to_core + forward:
        copy.wait_recv()
    for t in range(3):
        sent, keep = moved[t]
        keep.wait()
        for copy in sent:
            copy.wait_recv()

    def block_inputs(k, _):
        r = k * 2
        total = None
        for t in range(3):
            sides = [
                jnp.concatenate([gall[t, hd, h, r + s] for hd in range(4) for h in range(HEADS)], axis=0)
                for s in range(2)
            ]
            term = nn(wfull[t], jnp.concatenate(sides, axis=1))
            total = term if total is None else total + term
        flat = total.T.astype(BF16)
        gin_ref[r] = flat[:128]
        gin_ref[r + 1] = flat[128:]
        return 0

    lax.fori_loop(0, 2, block_inputs, 0)
    wgather_a[0].finish()
    wgather_a[1].finish()
    wt_ref[...] = wfin[...]
    copies.drain()


def body(inputs, out_grad, w_query, w_key, w_value, w_output):
    vmem = lambda *shape: pltpu.VMEM(shape, BF16)
    gin, wts = pl.pallas_call(
        kernel,
        out_shape=(
            jax.ShapeDtypeStruct((ROWS, 128, D), BF16),
            jax.ShapeDtypeStruct((2, 2 * WIDTH, D), BF16),
        ),
        in_specs=[pl.BlockSpec(memory_space=pl.ANY)] * 6,
        out_specs=(pl.BlockSpec(memory_space=pltpu.VMEM),) * 2,
        scratch_shapes=[
            vmem(ROWS, COLS, D),
            vmem(ROWS, COLS, D),
            vmem(WIDTH, D),
            vmem(3, D, 4 * WIDTH),
            vmem(3 * WIDTH, D),
            vmem(4, HEADS, ROWS * HEAD_DIM, COLS),
            vmem(2, HEADS, COLS, COLS),
            vmem(2, 2, 128, COLS),
            vmem(2, 2, 2, 128, COLS),
            vmem(2, 2, 128, COLS),
            vmem(2, HEADS, 128, COLS),
            vmem(2, 2, 32, COLS),
            vmem(2, 2, 2, 32, COLS),
            vmem(2, 2, 32, COLS),
            vmem(2, HEADS, 32, COLS),
            vmem(2, 3, 16, COLS),
            vmem(2, HEADS, COLS, COLS),
            vmem(HEADS, ROWS, HEAD_DIM, COLS),
            vmem(3, HEADS, ROWS, HEAD_DIM, COLS),
            vmem(3, 4, HEADS, ROWS, HEAD_DIM, 128),
            pltpu.VMEM((2 * WIDTH, D), F32),
            vmem(2, 2 * WIDTH, D),
            vmem(2, 2, 64, 384),
            vmem(2, 2, 2, 64, 384),
            vmem(2, 2, 64, 384),
            vmem(2, 64, D),
            vmem(2, 2, 16, 384),
            vmem(2, 2, 2, 16, 384),
            vmem(2, 2, 16, 384),
            vmem(2, 4, 16, D),
            vmem(2, 2 * WIDTH, D),
            pltpu.SemaphoreType.DMA((9,)),
            pltpu.SemaphoreType.DMA((COPIES,)),
            pltpu.SemaphoreType.DMA((COPIES,)),
        ],
        compiler_params=pltpu.CompilerParams(
            collective_id=0, has_side_effects=True, vmem_limit_bytes=56 * 1024 * 1024
        ),
        name="tied_row_attention_grad",
    )(inputs, out_grad, w_query, w_key, w_value, w_output)
    scaled = wts.astype(F32) * INV_ROOT
    turned = lambda w: w.T
    return (
        gin,
        turned(scaled[1, :WIDTH]),
        turned(scaled[1, WIDTH:]),
        turned(scaled[0, :WIDTH]),
        scaled[0, WIDTH:],
    )


def solution(mesh):
    finer = Mesh(mesh.devices.reshape(4, 4, 4, 2, 2), AXES)
    return jax.shard_map(
        body,
        mesh=finer,
        in_specs=(
            P(SEQ, None, None),
            P(SEQ, None, None),
            P(None, HEAD),
            P(None, HEAD),
            P(None, HEAD),
            P(HEAD, None),
        ),
        out_specs=(
            P(SEQ, HEAD, None),
            P(None, HEAD),
            P(None, HEAD),
            P(None, HEAD),
            P(HEAD, None),
        ),
        check_vma=False,
    )
```

```python
import math

import jax
import jax.numpy as jnp
from jax import lax
from jax.experimental import pallas as pl
from jax.experimental.pallas import tpu as pltpu
from jax.sharding import Mesh
from jax.sharding import PartitionSpec as P

AXES = ("y", "zh", "x", "zl", "core")
SEQ = ("y", "zh", "x")
HEAD = ("zl", "core")
ROWS, COLS, D, HEAD_DIM, HEADS = 4, 512, 768, 64, 2
WIDTH = HEADS * HEAD_DIM
ALL_ROWS = 256
C = 1.0 / (math.sqrt(HEAD_DIM) * math.sqrt(ALL_ROWS))
INV_ROOT = 1.0 / math.sqrt(ALL_ROWS * COLS)
COPIES = 176
F32, BF16 = jnp.float32, jnp.bfloat16


def nt(a, b):
    return lax.dot_general(a, b, (((1,), (1,)), ((), ())), preferred_element_type=F32)


def nn(a, b):
    return lax.dot_general(a, b, (((1,), (0,)), ((), ())), preferred_element_type=F32)


def tn(a, b):
    return lax.dot_general(a, b, (((0,), (0,)), ((), ())), preferred_element_type=F32)


class Copies:
    def __init__(self, send_sem, recv_sem):
        self.send_sem, self.recv_sem, self.made = send_sem, recv_sem, []

    def send(self, src, dst, device):
        k = len(self.made)
        copy = pltpu.make_async_remote_copy(
            src_ref=src,
            dst_ref=dst,
            send_sem=self.send_sem.at[k],
            recv_sem=self.recv_sem.at[k],
            device_id=device,
            device_id_type=pl.DeviceIdType.MESH,
        )
        copy.start()
        self.made.append(copy)
        return copy

    def drain(self):
        for copy in self.made:
            copy.wait_send()


class RingSum:
    def __init__(self, copies, piece, rel, rcv, tmp, right, left):
        self.copies, self.piece, self.rel, self.rcv, self.tmp = copies, piece, rel, rcv, tmp
        self.right, self.left = right, left

    def start_far(self):
        send, piece = self.copies.send, self.piece
        self.c1 = send(piece(2, 0), self.rel.at[0], self.right)
        self.c2 = send(piece(2, 1), self.rel.at[1], self.left)

    def start_near(self):
        send, piece = self.copies.send, self.piece
        self.c3 = send(piece(1, 1), self.rcv.at[0, 1], self.right)
        self.c4 = send(piece(3, 0), self.rcv.at[1, 0], self.left)

    def relay(self):
        send, piece = self.copies.send, self.piece
        self.c1.wait_recv()
        self.tmp[0] = (piece(1, 0)[...].astype(F32) + self.rel[0].astype(F32)).astype(BF16)
        self.c2.wait_recv()
        self.tmp[1] = (piece(3, 1)[...].astype(F32) + self.rel[1].astype(F32)).astype(BF16)
        self.c5 = send(self.tmp.at[0], self.rcv.at[0, 0], self.right)
        self.c6 = send(self.tmp.at[1], self.rcv.at[1, 1], self.left)

    def finish(self):
        for copy in (self.c3, self.c4, self.c5, self.c6):
            copy.wait_recv()
        return [
            self.piece(0, half)[...].astype(F32)
            + self.rcv[0, half].astype(F32)
            + self.rcv[1, half].astype(F32)
            for half in range(2)
        ]


class RingGather:
    def __init__(self, copies, block, right, left):
        self.copies, self.block, self.right, self.left = copies, block, right, left

    def start(self):
        whole = self.block(0, None)
        self.d1 = self.copies.send(whole, whole, self.right)
        self.d2 = self.copies.send(whole, whole, self.left)

    def relay(self):
        self.d1.wait_recv()
        far = self.block(3, 0)
        self.e1 = self.copies.send(far, far, self.right)
        self.d2.wait_recv()
        far = self.block(1, 1)
        self.e2 = self.copies.send(far, far, self.left)

    def finish(self):
        self.e1.wait_recv()
        self.e2.wait_recv()


def kernel(
    x_hbm, g_hbm, wq_hbm, wk_hbm, wv_hbm, wo_hbm,
    gin_ref, gq_ref, gk_ref, gv_ref, go_ref,
    xv, gv, wo, wfull, wt, proj, part,
    rel1, rcv1, tmp1, sum1, own1, rcv2, sum2, own2, rcv3,
    pd, att, grad, gall,
    wacc, wpart, wrcv1, wsum1, wrcv2, wrcv3, wfin,
    load_sem, send_sem, recv_sem,
):
    y, zh, x, zl, co = (lax.axis_index(n) for n in AXES)
    a = x * (1 - co) + y * co
    b = y * (1 - co) + x * co
    head = zl * 2 + co

    def dev(da=0, db=0, dc=0, dzl=0, dco=0):
        return (
            lax.rem(y + da * co + db * (1 - co), 4),
            lax.rem(zh + dc, 4),
            lax.rem(x + da * (1 - co) + db * co, 4),
            lax.rem(zl + dzl, 2),
            lax.rem(co + dco, 2),
        )

    a_to = [None] + [dev(da=k) for k in (1, 2, 3)]
    b_to = [None] + [dev(db=k) for k in (1, 2, 3)]
    z_to = [None] + [dev(dc=k) for k in (1, 2, 3)]
    h_core, h_chip, h_both = dev(dco=1), dev(dzl=1), dev(dzl=1, dco=1)
    near_first = (1, 3, 2)

    def rows_of(start, size):
        return pl.ds(pl.multiple_of(start, size), size)

    def place(at, off):
        return lax.rem(at + off, 4)

    mine = rows_of(head * WIDTH, WIDTH)
    loads = [
        pltpu.make_async_copy(w.at[...], wfull.at[t, :, mine], load_sem.at[t])
        for t, w in enumerate((wq_hbm, wk_hbm, wv_hbm))
    ]
    loads.append(pltpu.make_async_copy(x_hbm, xv, load_sem.at[3]))
    loads.append(pltpu.make_async_copy(wo_hbm, wo, load_sem.at[4]))
    loads.append(pltpu.make_async_copy(g_hbm, gv, load_sem.at[5]))
    for load in loads:
        load.start()

    barrier = pltpu.get_barrier_semaphore()
    friends = [*a_to[1:], *b_to[1:], *z_to[1:], h_core, h_chip, h_both]
    for friend in friends:
        pl.semaphore_signal(barrier, inc=1, device_id=friend, device_id_type=pl.DeviceIdType.MESH)

    copies = Copies(send_sem, recv_sem)
    for load in loads[:4]:
        load.wait()
    for t in range(3):
        wt[t * WIDTH : (t + 1) * WIDTH, :] = wfull[t, :, mine].T

    def project(r, _):
        res = nt(wt[...], xv[r]).astype(BF16)
        at = rows_of(r * HEAD_DIM, HEAD_DIM)
        for t in range(3):
            for h in range(HEADS):
                k = t * WIDTH + h * HEAD_DIM
                proj[t, h, at, :] = res[k : k + HEAD_DIM]
        return 0

    lax.fori_loop(0, ROWS, project, 0)

    def products(m, left, right):
        def one(k, _):
            h, blk = k // 4, lax.rem(k, 4)
            at = rows_of(blk * 128, 128)
            part[m, h, at, :] = tn(proj[left, h, :, at], proj[right, h]).astype(BF16)
            return 0

        lax.fori_loop(0, 4 * HEADS, one, 0)

    products(0, 0, 1)
    pl.semaphore_wait(barrier, len(friends))

    order = (2, 1, 3, 0)

    def ring1(m, k):
        def piece(off, half):
            return part.at[m, half, rows_of(place(a, off) * 128 + place(b, k) * 32, 32), :]

        return RingSum(copies, piece, rel1.at[m, k], rcv1.at[m, k], tmp1.at[m, k], a_to[1], a_to[3])

    first = [[ring1(m, k) for k in range(4)] for m in range(2)]

    def start_first(m):
        for k in order:
            first[m][k].start_far()
        for k in order:
            first[m][k].start_near()

    start_first(0)
    to_core = [copies.send(wfull.at[t, :, mine], wfull.at[t, :, mine], h_core) for t in range(3)]
    to_chip = [copies.send(wfull.at[t, :, mine], wfull.at[t, :, mine], h_chip) for t in range(3)]

    for load in loads[4:]:
        load.wait()

    def project_grad(r, _):
        res = nt(wo[...], gv[r]).astype(BF16)
        at = rows_of(r * HEAD_DIM, HEAD_DIM)
        for h in range(HEADS):
            proj[3, h, at, :] = res[h * HEAD_DIM : (h + 1) * HEAD_DIM]
        return 0

    lax.fori_loop(0, ROWS, project_grad, 0)
    for k in order:
        first[0][k].relay()
    products(1, 3, 2)
    start_first(1)

    second = [[None] * 4 for _ in range(2)]

    def end_first(m):
        for k in order:
            for half, total in enumerate(first[m][k].finish()):
                if k:
                    sum1[m, k - 1, half] = total.astype(BF16)
                else:
                    own1[m, half] = total
            if k:
                second[m][k] = copies.send(sum1.at[m, k - 1], rcv2.at[m, k - 1], b_to[k])

    def spot(off):
        at = place(zh, off)
        return at // 2, rows_of(lax.rem(at, 2) * 16, 16)

    third = [[None] * 4 for _ in range(2)]

    def end_second(m):
        total = own1[m]
        for k in near_first:
            second[m][k].wait_recv()
            total = total + rcv2[m, k - 1].astype(F32)
        sum2[m] = total.astype(BF16)
        own2[m] = total
        for k in (2, 1, 3):
            h, at = spot(k)
            third[m][k] = copies.send(sum2.at[m, h, at, :], rcv3.at[m, k - 1], z_to[k])

    end_first(0)
    for k in order:
        first[1][k].relay()
    end_second(0)
    end_first(1)

    theirs = rows_of((lax.rem(zl + 1, 2) * 2 + co) * WIDTH, WIDTH)
    forward = []
    for t in range(3):
        to_chip[t].wait_recv()
        forward.append(copies.send(wfull.at[t, :, theirs], wfull.at[t, :, theirs], h_core))
    end_second(1)

    def end_third(m):
        h, at = spot(0)
        total = own2[m, h, at, :]
        for k in near_first:
            third[m][k].wait_recv()
            total = total + rcv3[m, k - 1].astype(F32)
        return total

    exponent = jnp.exp(C * end_third(0))
    probs = exponent / jnp.sum(exponent, axis=1, keepdims=True)
    own_h, _ = spot(0)
    own_rows = rows_of(a * 128 + b * 32 + lax.rem(zh, 2) * 16, 16)
    pd[0, own_h, own_rows, :] = probs.astype(BF16)
    grad_probs = end_third(1)
    inner = jnp.sum(probs * grad_probs, axis=1, keepdims=True)
    pd[1, own_h, own_rows, :] = (C * probs * (grad_probs - inner)).astype(BF16)
    spread = [[], []]
    for m in range(2):
        own = pd.at[m, own_h, own_rows, :]
        spread[m] = [copies.send(own, own, z_to[k]) for k in (2, 1, 3)]

    def block(m, k):
        def at(off, half):
            rows = rows_of(place(a, off) * 128 + place(b, k) * 32, 32)
            return pd.at[m, :, rows, :] if half is None else pd.at[m, half, rows, :]

        return at

    gather_a = [
        [RingGather(copies, block(m, k), a_to[1], a_to[3]) for k in range(4)] for m in range(2)
    ]
    gather_b = [[None] * 4 for _ in range(2)]
    for m in range(2):
        for copy in spread[m]:
            copy.wait_recv()
        own = block(m, 0)(0, None)
        for k in (2, 1, 3):
            gather_b[m][k] = copies.send(own, own, b_to[k])
        gather_a[m][0].start()

    def pass_on(m, k):
        gather_b[m][(4 - k) % 4].wait_recv()
        gather_a[m][k].start()

    gather_a[0][0].relay()
    for m in range(2):
        for k in near_first:
            pass_on(m, k)
        if m == 0:
            gather_a[1][0].relay()
    for m in range(2):
        for k in near_first:
            gather_a[m][k].relay()

    def pair_value(h, _):
        p = pd[0, h]
        att[h] = nt(proj[2, h], p).astype(BF16).reshape(ROWS, HEAD_DIM, COLS)
        grad[2, h] = nn(proj[3, h], p).astype(BF16).reshape(ROWS, HEAD_DIM, COLS)
        return 0

    def pair_score(h, _):
        d = pd[1, h]
        grad[0, h] = nt(proj[1, h], d).astype(BF16).reshape(ROWS, HEAD_DIM, COLS)
        grad[1, h] = nn(proj[0, h], d).astype(BF16).reshape(ROWS, HEAD_DIM, COLS)
        return 0

    def to_heads(t):
        sent = []
        for device, dzl, dco in ((h_chip, 1, 0), (h_both, 1, 1), (h_core, 0, 1)):
            at = rows_of((lax.rem(zl + dzl, 2) * 2 + lax.rem(co + dco, 2)) * 128, 128)
            sent.append(copies.send(grad.at[t, :, :, :, at], gall.at[t, head], device))
        keep = pltpu.make_async_copy(grad.at[t, :, :, :, mine], gall.at[t, head], load_sem.at[6 + t])
        keep.start()
        return sent, keep

    def weight_part(p, kinds):
        def one(r, _):
            for k, (source, t) in enumerate(kinds):
                src = att if t is None else grad.at[t]
                lhs = jnp.concatenate([src[0, r], src[1, r]], axis=0)
                at = slice(k * WIDTH, (k + 1) * WIDTH)
                wacc[at, :] = jnp.where(r == 0, 0.0, wacc[at, :]) + nn(lhs, source[r])
            return 0

        lax.fori_loop(0, ROWS, one, 0)
        wpart[p] = wacc[...].astype(BF16)

    wfirst = [[None] * 4 for _ in range(2)]
    wsecond = [[None] * 4 for _ in range(2)]
    wthird = [[None] * 4 for _ in range(2)]

    def start_weights(p):
        for k in (2, 1, 3):
            wfirst[p][k] = copies.send(
                wpart.at[p, rows_of(place(a, k) * 64, 64), :], wrcv1.at[p, k - 1], a_to[k]
            )

    def end_wfirst(p):
        total = wpart[p, rows_of(a * 64, 64), :].astype(F32)
        for k in near_first:
            wfirst[p][k].wait_recv()
            total = total + wrcv1[p, k - 1].astype(F32)
        wsum1[p] = total.astype(BF16)
        for k in (2, 1, 3):
            wsecond[p][k] = copies.send(
                wsum1.at[p, rows_of(place(b, k) * 16, 16), :], wrcv2.at[p, k - 1], b_to[k]
            )

    def end_wsecond(p):
        total = wsum1[p, rows_of(b * 16, 16), :].astype(F32)
        for k in near_first:
            wsecond[p][k].wait_recv()
            total = total + wrcv2[p, k - 1].astype(F32)
        wrcv3[p, zh] = total.astype(BF16)
        own = wrcv3.at[p, zh]
        for k in (2, 1, 3):
            wthird[p][k] = copies.send(own, own, z_to[k])

    wgather_b = [[None] * 4 for _ in range(2)]
    wgather_a = [[], []]

    def wblock(p, k):
        return wfin.at[p, rows_of(a * 64 + place(b, k) * 16, 16), :]

    def spread_weights(p, k):
        own = wblock(p, k)
        for d in (2, 1, 3):
            wgather_a[p].append(copies.send(own, own, a_to[d]))

    def end_wthird(p):
        for k in near_first:
            wthird[p][k].wait_recv()
        total = wrcv3[p, 0].astype(F32) + wrcv3[p, 1].astype(F32)
        total = total + wrcv3[p, 2].astype(F32) + wrcv3[p, 3].astype(F32)
        wfin[p, rows_of(a * 64 + b * 16, 16), :] = total.astype(BF16)
        own = wblock(p, 0)
        for k in (2, 1, 3):
            wgather_b[p][k] = copies.send(own, own, b_to[k])
        spread_weights(p, 0)

    def pass_on_weights(p):
        for k in near_first:
            wgather_b[p][(4 - k) % 4].wait_recv()
            spread_weights(p, k)

    for k in range(4):
        gather_a[0][k].finish()
    lax.fori_loop(0, HEADS, pair_value, 0)
    moved = {2: to_heads(2)}
    weight_part(0, ((xv, 2), (gv, None)))
    start_weights(0)
    for k in range(4):
        gather_a[1][k].finish()
    lax.fori_loop(0, HEADS, pair_score, 0)
    moved[0] = to_heads(0)
    moved[1] = to_heads(1)
    weight_part(1, ((xv, 0), (xv, 1)))
    start_weights(1)
    end_wfirst(0)
    end_wsecond(0)
    end_wfirst(1)
    end_wsecond(1)
    end_wthird(0)
    pass_on_weights(0)
    end_wthird(1)

    for copy in to_core + forward:
        copy.wait_recv()
    for t in range(3):
        sent, keep = moved[t]
        keep.wait()
        for copy in sent:
            copy.wait_recv()
    pass_on_weights(1)

    def block_inputs(k, _):
        r = k * 2
        total = None
        for t in range(3):
            sides = [
                jnp.concatenate([gall[t, hd, h, r + s] for hd in range(4) for h in range(HEADS)], axis=0)
                for s in range(2)
            ]
            term = nn(wfull[t], jnp.concatenate(sides, axis=1))
            total = term if total is None else total + term
        flat = total.T.astype(BF16)
        gin_ref[r] = flat[:128]
        gin_ref[r + 1] = flat[128:]
        return 0

    lax.fori_loop(0, 2, block_inputs, 0)
    for p in range(2):
        for copy in wgather_a[p]:
            copy.wait_recv()
    gv_ref[...] = wfin[0, :WIDTH].T
    go_ref[...] = wfin[0, WIDTH:]
    gq_ref[...] = wfin[1, :WIDTH].T
    gk_ref[...] = wfin[1, WIDTH:].T
    copies.drain()


def body(inputs, out_grad, w_query, w_key, w_value, w_output):
    vmem = lambda *shape: pltpu.VMEM(shape, BF16)
    gin, gq, gk, gv, go = pl.pallas_call(
        kernel,
        out_shape=(
            jax.ShapeDtypeStruct((ROWS, 128, D), BF16),
            *(jax.ShapeDtypeStruct((D, WIDTH), BF16) for _ in range(3)),
            jax.ShapeDtypeStruct((WIDTH, D), BF16),
        ),
        in_specs=[pl.BlockSpec(memory_space=pl.ANY)] * 6,
        out_specs=(pl.BlockSpec(memory_space=pltpu.VMEM),) * 5,
        scratch_shapes=[
            vmem(ROWS, COLS, D),
            vmem(ROWS, COLS, D),
            vmem(WIDTH, D),
            vmem(3, D, 4 * WIDTH),
            vmem(3 * WIDTH, D),
            vmem(4, HEADS, ROWS * HEAD_DIM, COLS),
            vmem(2, HEADS, COLS, COLS),
            vmem(2, 4, 2, 32, COLS),
            vmem(2, 4, 2, 2, 32, COLS),
            vmem(2, 4, 2, 32, COLS),
            vmem(2, 3, HEADS, 32, COLS),
            pltpu.VMEM((2, HEADS, 32, COLS), F32),
            vmem(2, 3, HEADS, 32, COLS),
            vmem(2, HEADS, 32, COLS),
            pltpu.VMEM((2, HEADS, 32, COLS), F32),
            vmem(2, 3, 16, COLS),
            vmem(2, HEADS, COLS, COLS),
            vmem(HEADS, ROWS, HEAD_DIM, COLS),
            vmem(3, HEADS, ROWS, HEAD_DIM, COLS),
            vmem(3, 4, HEADS, ROWS, HEAD_DIM, 128),
            pltpu.VMEM((2 * WIDTH, D), F32),
            vmem(2, 2 * WIDTH, D),
            vmem(2, 3, 64, D),
            vmem(2, 64, D),
            vmem(2, 3, 16, D),
            vmem(2, 4, 16, D),
            vmem(2, 2 * WIDTH, D),
            pltpu.SemaphoreType.DMA((9,)),
            pltpu.SemaphoreType.DMA((COPIES,)),
            pltpu.SemaphoreType.DMA((COPIES,)),
        ],
        compiler_params=pltpu.CompilerParams(
            collective_id=0, has_side_effects=True, vmem_limit_bytes=56 * 1024 * 1024
        ),
        name="tied_row_attention_grad",
    )(inputs, out_grad, w_query, w_key, w_value, w_output)
    scaled = lambda w: w.astype(F32) * INV_ROOT
    return gin, scaled(gq), scaled(gk), scaled(gv), scaled(go)


def solution(mesh):
    finer = Mesh(mesh.devices.reshape(4, 4, 4, 2, 2), AXES)
    return jax.shard_map(
        body,
        mesh=finer,
        in_specs=(
            P(SEQ, None, None),
            P(SEQ, None, None),
            P(None, HEAD),
            P(None, HEAD),
            P(None, HEAD),
            P(HEAD, None),
        ),
        out_specs=(
            P(SEQ, HEAD, None),
            P(None, HEAD),
            P(None, HEAD),
            P(None, HEAD),
            P(HEAD, None),
        ),
        check_vma=False,
    )
```

```python
import math

import jax
import jax.numpy as jnp
from jax import lax
from jax.experimental import pallas as pl
from jax.experimental.pallas import tpu as pltpu
from jax.sharding import Mesh
from jax.sharding import PartitionSpec as P

AXES = ("y", "zh", "x", "zl", "core")
SEQ = ("y", "zh", "x")
HEAD = ("zl", "core")
ROWS, COLS, D, HEAD_DIM, HEADS = 4, 512, 768, 64, 2
WIDTH = HEADS * HEAD_DIM
ALL_ROWS = 256
C = 1.0 / (math.sqrt(HEAD_DIM) * math.sqrt(ALL_ROWS))
INV_ROOT = 1.0 / math.sqrt(ALL_ROWS * COLS)
COPIES = 176
F32, BF16 = jnp.float32, jnp.bfloat16


def nt(a, b):
    return lax.dot_general(a, b, (((1,), (1,)), ((), ())), preferred_element_type=F32)


def nn(a, b):
    return lax.dot_general(a, b, (((1,), (0,)), ((), ())), preferred_element_type=F32)


def tn(a, b):
    return lax.dot_general(a, b, (((0,), (0,)), ((), ())), preferred_element_type=F32)


class Copies:
    def __init__(self, send_sem, recv_sem):
        self.send_sem, self.recv_sem, self.made = send_sem, recv_sem, []

    def send(self, src, dst, device):
        k = len(self.made)
        copy = pltpu.make_async_remote_copy(
            src_ref=src,
            dst_ref=dst,
            send_sem=self.send_sem.at[k],
            recv_sem=self.recv_sem.at[k],
            device_id=device,
            device_id_type=pl.DeviceIdType.MESH,
        )
        copy.start()
        self.made.append(copy)
        return copy

    def drain(self):
        for copy in self.made:
            copy.wait_send()


class RingSum:
    def __init__(self, copies, piece, rel, rcv, tmp, right, left):
        self.copies, self.piece, self.rel, self.rcv, self.tmp = copies, piece, rel, rcv, tmp
        self.right, self.left = right, left

    def start_far(self):
        send, piece = self.copies.send, self.piece
        self.c1 = send(piece(2, 0), self.rel.at[0], self.right)
        self.c2 = send(piece(2, 1), self.rel.at[1], self.left)

    def start_near(self):
        send, piece = self.copies.send, self.piece
        self.c3 = send(piece(1, 1), self.rcv.at[0, 1], self.right)
        self.c4 = send(piece(3, 0), self.rcv.at[1, 0], self.left)

    def relay(self):
        send, piece = self.copies.send, self.piece
        self.c1.wait_recv()
        self.tmp[0] = (piece(1, 0)[...].astype(F32) + self.rel[0].astype(F32)).astype(BF16)
        self.c2.wait_recv()
        self.tmp[1] = (piece(3, 1)[...].astype(F32) + self.rel[1].astype(F32)).astype(BF16)
        self.c5 = send(self.tmp.at[0], self.rcv.at[0, 0], self.right)
        self.c6 = send(self.tmp.at[1], self.rcv.at[1, 1], self.left)

    def finish(self):
        for copy in (self.c3, self.c4, self.c5, self.c6):
            copy.wait_recv()
        return [
            self.piece(0, half)[...].astype(F32)
            + self.rcv[0, half].astype(F32)
            + self.rcv[1, half].astype(F32)
            for half in range(2)
        ]


class RingGather:
    def __init__(self, copies, block, right, left):
        self.copies, self.block, self.right, self.left = copies, block, right, left

    def start(self):
        whole = self.block(0, None)
        self.d1 = self.copies.send(whole, whole, self.right)
        self.d2 = self.copies.send(whole, whole, self.left)

    def relay(self):
        self.d1.wait_recv()
        far = self.block(3, 0)
        self.e1 = self.copies.send(far, far, self.right)
        self.d2.wait_recv()
        far = self.block(1, 1)
        self.e2 = self.copies.send(far, far, self.left)

    def finish(self):
        self.e1.wait_recv()
        self.e2.wait_recv()


def kernel(
    x_hbm, g_hbm, wq_hbm, wk_hbm, wv_hbm, wo_hbm,
    gin_ref, gq_ref, gk_ref, gv_ref, go_ref,
    xv, gv, wo, wfull, wt, proj, part,
    rel1, rcv1, tmp1, sum1, own1, rcv2, sum2, own2, rcv3,
    pd, att, grad, gall,
    wacc, wpart, wrcv1, wsum1, wrcv2, wrcv3, wfin,
    load_sem, send_sem, recv_sem,
):
    y, zh, x, zl, co = (lax.axis_index(n) for n in AXES)
    a = x * (1 - co) + y * co
    b = y * (1 - co) + x * co
    head = zl * 2 + co

    def dev(da=0, db=0, dc=0, dzl=0, dco=0):
        return (
            lax.rem(y + da * co + db * (1 - co), 4),
            lax.rem(zh + dc, 4),
            lax.rem(x + da * (1 - co) + db * co, 4),
            lax.rem(zl + dzl, 2),
            lax.rem(co + dco, 2),
        )

    a_to = [None] + [dev(da=k) for k in (1, 2, 3)]
    b_to = [None] + [dev(db=k) for k in (1, 2, 3)]
    z_to = [None] + [dev(dc=k) for k in (1, 2, 3)]
    h_core, h_chip, h_both = dev(dco=1), dev(dzl=1), dev(dzl=1, dco=1)
    near_first = (1, 3, 2)

    def rows_of(start, size):
        return pl.ds(pl.multiple_of(start, size), size)

    def place(at, off):
        return lax.rem(at + off, 4)

    mine = rows_of(head * WIDTH, WIDTH)
    loads = [
        pltpu.make_async_copy(w.at[...], wfull.at[t, :, mine], load_sem.at[t])
        for t, w in enumerate((wq_hbm, wk_hbm, wv_hbm))
    ]
    loads.append(pltpu.make_async_copy(x_hbm, xv, load_sem.at[3]))
    loads.append(pltpu.make_async_copy(wo_hbm, wo, load_sem.at[4]))
    loads.append(pltpu.make_async_copy(g_hbm, gv, load_sem.at[5]))
    for load in loads[:4]:
        load.start()

    barrier = pltpu.get_barrier_semaphore()
    friends = [*a_to[1:], *b_to[1:], *z_to[1:], h_core, h_chip, h_both]
    for friend in friends:
        pl.semaphore_signal(barrier, inc=1, device_id=friend, device_id_type=pl.DeviceIdType.MESH)

    copies = Copies(send_sem, recv_sem)
    for load in loads[:3]:
        load.wait()
    for load in loads[4:]:
        load.start()
    for t in range(3):
        wt[t * WIDTH : (t + 1) * WIDTH, :] = wfull[t, :, mine].T

    loads[3].wait()

    def project(r, _):
        res = nt(wt[...], xv[r]).astype(BF16)
        at = rows_of(r * HEAD_DIM, HEAD_DIM)
        for t in range(3):
            for h in range(HEADS):
                k = t * WIDTH + h * HEAD_DIM
                proj[t, h, at, :] = res[k : k + HEAD_DIM]
        return 0

    lax.fori_loop(0, ROWS, project, 0)

    def products(m, left, right):
        def one(k, _):
            h, blk = k // 4, lax.rem(k, 4)
            at = rows_of(blk * 128, 128)
            part[m, h, at, :] = tn(proj[left, h, :, at], proj[right, h]).astype(BF16)
            return 0

        lax.fori_loop(0, 4 * HEADS, one, 0)

    products(0, 0, 1)
    pl.semaphore_wait(barrier, len(friends))

    order = (2, 1, 3, 0)

    def ring1(m, k):
        def piece(off, half):
            return part.at[m, half, rows_of(place(a, off) * 128 + place(b, k) * 32, 32), :]

        return RingSum(copies, piece, rel1.at[m, k], rcv1.at[m, k], tmp1.at[m, k], a_to[1], a_to[3])

    first = [[ring1(m, k) for k in range(4)] for m in range(2)]

    def start_first(m):
        for k in order:
            first[m][k].start_far()
        for k in order:
            first[m][k].start_near()

    start_first(0)
    for load in loads[4:]:
        load.wait()

    def project_grad(r, _):
        res = nt(wo[...], gv[r]).astype(BF16)
        at = rows_of(r * HEAD_DIM, HEAD_DIM)
        for h in range(HEADS):
            proj[3, h, at, :] = res[h * HEAD_DIM : (h + 1) * HEAD_DIM]
        return 0

    lax.fori_loop(0, ROWS, project_grad, 0)
    for k in order:
        first[0][k].relay()
    products(1, 3, 2)
    start_first(1)

    second = [[None] * 4 for _ in range(2)]

    def end_first(m):
        for k in order:
            for half, total in enumerate(first[m][k].finish()):
                if k:
                    sum1[m, k - 1, half] = total.astype(BF16)
                else:
                    own1[m, half] = total
            if k:
                second[m][k] = copies.send(sum1.at[m, k - 1], rcv2.at[m, k - 1], b_to[k])

    def spot(off):
        at = place(zh, off)
        return at // 2, rows_of(lax.rem(at, 2) * 16, 16)

    third = [[None] * 4 for _ in range(2)]

    def end_second(m):
        total = own1[m]
        for k in near_first:
            second[m][k].wait_recv()
            total = total + rcv2[m, k - 1].astype(F32)
        sum2[m] = total.astype(BF16)
        own2[m] = total
        for k in (2, 1, 3):
            h, at = spot(k)
            third[m][k] = copies.send(sum2.at[m, h, at, :], rcv3.at[m, k - 1], z_to[k])

    end_first(0)
    for k in order:
        first[1][k].relay()
    end_second(0)
    end_first(1)

    end_second(1)

    def end_third(m):
        h, at = spot(0)
        total = own2[m, h, at, :]
        for k in near_first:
            third[m][k].wait_recv()
            total = total + rcv3[m, k - 1].astype(F32)
        return total

    exponent = jnp.exp(C * end_third(0))
    probs = exponent / jnp.sum(exponent, axis=1, keepdims=True)
    own_h, _ = spot(0)
    own_rows = rows_of(a * 128 + b * 32 + lax.rem(zh, 2) * 16, 16)
    pd[0, own_h, own_rows, :] = probs.astype(BF16)
    grad_probs = end_third(1)
    inner = jnp.sum(probs * grad_probs, axis=1, keepdims=True)
    pd[1, own_h, own_rows, :] = (C * probs * (grad_probs - inner)).astype(BF16)
    spread = [[], []]
    for m in range(2):
        own = pd.at[m, own_h, own_rows, :]
        spread[m] = [copies.send(own, own, z_to[k]) for k in (2, 1, 3)]

    def block(m, k):
        def at(off, half):
            rows = rows_of(place(a, off) * 128 + place(b, k) * 32, 32)
            return pd.at[m, :, rows, :] if half is None else pd.at[m, half, rows, :]

        return at

    gather_a = [
        [RingGather(copies, block(m, k), a_to[1], a_to[3]) for k in range(4)] for m in range(2)
    ]
    gather_b = [[None] * 4 for _ in range(2)]
    for m in range(2):
        for copy in spread[m]:
            copy.wait_recv()
        own = block(m, 0)(0, None)
        for k in (2, 1, 3):
            gather_b[m][k] = copies.send(own, own, b_to[k])
        gather_a[m][0].start()

    to_core = [copies.send(wfull.at[t, :, mine], wfull.at[t, :, mine], h_core) for t in range(3)]
    to_chip = [copies.send(wfull.at[t, :, mine], wfull.at[t, :, mine], h_chip) for t in range(3)]

    def pass_on(m, k):
        gather_b[m][(4 - k) % 4].wait_recv()
        gather_a[m][k].start()

    gather_a[0][0].relay()
    for m in range(2):
        for k in near_first:
            pass_on(m, k)
        if m == 0:
            gather_a[1][0].relay()
    for m in range(2):
        for k in near_first:
            gather_a[m][k].relay()

    def pair_value(h, _):
        p = pd[0, h]
        att[h] = nt(proj[2, h], p).astype(BF16).reshape(ROWS, HEAD_DIM, COLS)
        grad[2, h] = nn(proj[3, h], p).astype(BF16).reshape(ROWS, HEAD_DIM, COLS)
        return 0

    def pair_score(h, _):
        d = pd[1, h]
        grad[0, h] = nt(proj[1, h], d).astype(BF16).reshape(ROWS, HEAD_DIM, COLS)
        grad[1, h] = nn(proj[0, h], d).astype(BF16).reshape(ROWS, HEAD_DIM, COLS)
        return 0

    def to_heads(t):
        sent = []
        for device, dzl, dco in ((h_chip, 1, 0), (h_both, 1, 1), (h_core, 0, 1)):
            at = rows_of((lax.rem(zl + dzl, 2) * 2 + lax.rem(co + dco, 2)) * 128, 128)
            sent.append(copies.send(grad.at[t, :, :, :, at], gall.at[t, head], device))
        keep = pltpu.make_async_copy(grad.at[t, :, :, :, mine], gall.at[t, head], load_sem.at[6 + t])
        keep.start()
        return sent, keep

    def weight_part(p, kinds):
        def one(r, _):
            for k, (source, t) in enumerate(kinds):
                src = att if t is None else grad.at[t]
                lhs = jnp.concatenate([src[0, r], src[1, r]], axis=0)
                at = slice(k * WIDTH, (k + 1) * WIDTH)
                wacc[at, :] = jnp.where(r == 0, 0.0, wacc[at, :]) + nn(lhs, source[r])
            return 0

        lax.fori_loop(0, ROWS, one, 0)
        wpart[p] = wacc[...].astype(BF16)

    wfirst = [[None] * 4 for _ in range(2)]
    wsecond = [[None] * 4 for _ in range(2)]
    wthird = [[None] * 4 for _ in range(2)]

    def start_weights(p):
        for k in (2, 1, 3):
            wfirst[p][k] = copies.send(
                wpart.at[p, rows_of(place(a, k) * 64, 64), :], wrcv1.at[p, k - 1], a_to[k]
            )

    def end_wfirst(p):
        total = wpart[p, rows_of(a * 64, 64), :].astype(F32)
        for k in near_first:
            wfirst[p][k].wait_recv()
            total = total + wrcv1[p, k - 1].astype(F32)
        wsum1[p] = total.astype(BF16)
        for k in (2, 1, 3):
            wsecond[p][k] = copies.send(
                wsum1.at[p, rows_of(place(b, k) * 16, 16), :], wrcv2.at[p, k - 1], b_to[k]
            )

    def end_wsecond(p):
        total = wsum1[p, rows_of(b * 16, 16), :].astype(F32)
        for k in near_first:
            wsecond[p][k].wait_recv()
            total = total + wrcv2[p, k - 1].astype(F32)
        wrcv3[p, zh] = total.astype(BF16)
        own = wrcv3.at[p, zh]
        for k in (2, 1, 3):
            wthird[p][k] = copies.send(own, own, z_to[k])

    wgather_b = [[None] * 4 for _ in range(2)]
    wgather_a = [[], []]

    def wblock(p, k):
        return wfin.at[p, rows_of(a * 64 + place(b, k) * 16, 16), :]

    def spread_weights(p, k):
        own = wblock(p, k)
        for d in (2, 1, 3):
            wgather_a[p].append(copies.send(own, own, a_to[d]))

    def end_wthird(p):
        for k in near_first:
            wthird[p][k].wait_recv()
        total = wrcv3[p, 0].astype(F32) + wrcv3[p, 1].astype(F32)
        total = total + wrcv3[p, 2].astype(F32) + wrcv3[p, 3].astype(F32)
        wfin[p, rows_of(a * 64 + b * 16, 16), :] = total.astype(BF16)
        own = wblock(p, 0)
        for k in (2, 1, 3):
            wgather_b[p][k] = copies.send(own, own, b_to[k])
        spread_weights(p, 0)

    def pass_on_weights(p):
        for k in near_first:
            wgather_b[p][(4 - k) % 4].wait_recv()
            spread_weights(p, k)

    theirs = rows_of((lax.rem(zl + 1, 2) * 2 + co) * WIDTH, WIDTH)
    forward = []
    for t in range(3):
        to_chip[t].wait_recv()
        forward.append(copies.send(wfull.at[t, :, theirs], wfull.at[t, :, theirs], h_core))
    for k in range(4):
        gather_a[0][k].finish()
    lax.fori_loop(0, HEADS, pair_value, 0)
    moved = {2: to_heads(2)}
    weight_part(0, ((xv, 2), (gv, None)))
    start_weights(0)
    for k in range(4):
        gather_a[1][k].finish()
    lax.fori_loop(0, HEADS, pair_score, 0)
    moved[0] = to_heads(0)
    moved[1] = to_heads(1)
    weight_part(1, ((xv, 0), (xv, 1)))
    start_weights(1)
    end_wfirst(0)
    end_wsecond(0)
    end_wfirst(1)
    end_wsecond(1)
    end_wthird(0)
    pass_on_weights(0)
    end_wthird(1)

    for copy in to_core + forward:
        copy.wait_recv()
    for t in range(3):
        sent, keep = moved[t]
        keep.wait()
        for copy in sent:
            copy.wait_recv()
    pass_on_weights(1)

    def block_inputs(k, _):
        r = k * 2
        total = None
        for t in range(3):
            sides = [
                jnp.concatenate([gall[t, hd, h, r + s] for hd in range(4) for h in range(HEADS)], axis=0)
                for s in range(2)
            ]
            term = nn(wfull[t], jnp.concatenate(sides, axis=1))
            total = term if total is None else total + term
        flat = total.T.astype(BF16)
        gin_ref[r] = flat[:128]
        gin_ref[r + 1] = flat[128:]
        return 0

    lax.fori_loop(0, 2, block_inputs, 0)
    for p in range(2):
        for copy in wgather_a[p]:
            copy.wait_recv()
    gv_ref[...] = wfin[0, :WIDTH].T
    go_ref[...] = wfin[0, WIDTH:]
    gq_ref[...] = wfin[1, :WIDTH].T
    gk_ref[...] = wfin[1, WIDTH:].T
    copies.drain()


def last_step(*refs):
    sources, outs, held, made, sem = refs[:5], refs[5:10], refs[10:15], refs[15:19], refs[19]
    into = [pltpu.make_async_copy(sources[k], held[k], sem.at[k]) for k in range(5)]
    back = [pltpu.make_async_copy(held[0] if k == 0 else made[k - 1], outs[k], sem.at[5 + k]) for k in range(5)]
    for copy in into:
        copy.start()
    for k in range(5):
        into[k].wait()
        if k:
            made[k - 1][...] = held[k][...].astype(F32) * INV_ROOT
        back[k].start()
    for copy in back:
        copy.wait()


def body(inputs, out_grad, w_query, w_key, w_value, w_output):
    vmem = lambda *shape: pltpu.VMEM(shape, BF16)
    gin, gq, gk, gv, go = pl.pallas_call(
        kernel,
        out_shape=(
            jax.ShapeDtypeStruct((ROWS, 128, D), BF16),
            *(jax.ShapeDtypeStruct((D, WIDTH), BF16) for _ in range(3)),
            jax.ShapeDtypeStruct((WIDTH, D), BF16),
        ),
        in_specs=[pl.BlockSpec(memory_space=pltpu.HBM)] * 6,
        out_specs=(pl.BlockSpec(memory_space=pltpu.VMEM),) * 5,
        scratch_shapes=[
            vmem(ROWS, COLS, D),
            vmem(ROWS, COLS, D),
            vmem(WIDTH, D),
            vmem(3, D, 4 * WIDTH),
            vmem(3 * WIDTH, D),
            vmem(4, HEADS, ROWS * HEAD_DIM, COLS),
            vmem(2, HEADS, COLS, COLS),
            vmem(2, 4, 2, 32, COLS),
            vmem(2, 4, 2, 2, 32, COLS),
            vmem(2, 4, 2, 32, COLS),
            vmem(2, 3, HEADS, 32, COLS),
            pltpu.VMEM((2, HEADS, 32, COLS), F32),
            vmem(2, 3, HEADS, 32, COLS),
            vmem(2, HEADS, 32, COLS),
            pltpu.VMEM((2, HEADS, 32, COLS), F32),
            vmem(2, 3, 16, COLS),
            vmem(2, HEADS, COLS, COLS),
            vmem(HEADS, ROWS, HEAD_DIM, COLS),
            vmem(3, HEADS, ROWS, HEAD_DIM, COLS),
            vmem(3, 4, HEADS, ROWS, HEAD_DIM, 128),
            pltpu.VMEM((2 * WIDTH, D), F32),
            vmem(2, 2 * WIDTH, D),
            vmem(2, 3, 64, D),
            vmem(2, 64, D),
            vmem(2, 3, 16, D),
            vmem(2, 4, 16, D),
            vmem(2, 2 * WIDTH, D),
            pltpu.SemaphoreType.DMA((9,)),
            pltpu.SemaphoreType.DMA((COPIES,)),
            pltpu.SemaphoreType.DMA((COPIES,)),
        ],
        compiler_params=pltpu.CompilerParams(
            collective_id=0, has_side_effects=True, vmem_limit_bytes=56 * 1024 * 1024
        ),
        name="tied_row_attention_grad",
    )(inputs, out_grad, w_query, w_key, w_value, w_output)
    return pl.pallas_call(
        last_step,
        out_shape=(
            jax.ShapeDtypeStruct((ROWS, 128, D), BF16),
            *(jax.ShapeDtypeStruct((D, WIDTH), F32) for _ in range(3)),
            jax.ShapeDtypeStruct((WIDTH, D), F32),
        ),
        in_specs=[pl.BlockSpec(memory_space=pl.ANY)] * 5,
        out_specs=(pl.BlockSpec(memory_space=pl.ANY),) * 5,
        scratch_shapes=[
            vmem(ROWS, 128, D),
            *(vmem(D, WIDTH) for _ in range(3)),
            vmem(WIDTH, D),
            *(pltpu.VMEM((D, WIDTH), F32) for _ in range(3)),
            pltpu.VMEM((WIDTH, D), F32),
            pltpu.SemaphoreType.DMA((10,)),
        ],
        compiler_params=pltpu.CompilerParams(vmem_limit_bytes=60 * 1024 * 1024),
        name="scale_weight_grads",
    )(gin, gq, gk, gv, go)


def solution(mesh):
    finer = Mesh(mesh.devices.reshape(4, 4, 4, 2, 2), AXES)
    return jax.shard_map(
        body,
        mesh=finer,
        in_specs=(
            P(SEQ, None, None),
            P(SEQ, None, None),
            P(None, HEAD),
            P(None, HEAD),
            P(None, HEAD),
            P(HEAD, None),
        ),
        out_specs=(
            P(SEQ, HEAD, None),
            P(None, HEAD),
            P(None, HEAD),
            P(None, HEAD),
            P(HEAD, None),
        ),
        check_vma=False,
    )
```

```python
import math

import jax
import jax.numpy as jnp
from jax import lax
from jax.experimental import pallas as pl
from jax.experimental.pallas import tpu as pltpu
from jax.sharding import Mesh
from jax.sharding import PartitionSpec as P

AXES = ("y", "zh", "x", "zl", "core")
SEQ = ("y", "zh", "x")
HEAD = ("zl", "core")
ROWS, COLS, D, HEAD_DIM, HEADS = 4, 512, 768, 64, 2
WIDTH = HEADS * HEAD_DIM
ALL_ROWS = 256
C = 1.0 / (math.sqrt(HEAD_DIM) * math.sqrt(ALL_ROWS))
INV_ROOT = 1.0 / math.sqrt(ALL_ROWS * COLS)
COPIES = 176
F32, BF16 = jnp.float32, jnp.bfloat16


def nt(a, b):
    return lax.dot_general(a, b, (((1,), (1,)), ((), ())), preferred_element_type=F32)


def nn(a, b):
    return lax.dot_general(a, b, (((1,), (0,)), ((), ())), preferred_element_type=F32)


def tn(a, b):
    return lax.dot_general(a, b, (((0,), (0,)), ((), ())), preferred_element_type=F32)


class Copies:
    def __init__(self, send_sem, recv_sem):
        self.send_sem, self.recv_sem, self.made = send_sem, recv_sem, []

    def send(self, src, dst, device):
        k = len(self.made)
        copy = pltpu.make_async_remote_copy(
            src_ref=src,
            dst_ref=dst,
            send_sem=self.send_sem.at[k],
            recv_sem=self.recv_sem.at[k],
            device_id=device,
            device_id_type=pl.DeviceIdType.MESH,
        )
        copy.start()
        self.made.append(copy)
        return copy

    def drain(self):
        for copy in self.made:
            copy.wait_send()


class RingSum:
    def __init__(self, copies, piece, rel, rcv, tmp, right, left):
        self.copies, self.piece, self.rel, self.rcv, self.tmp = copies, piece, rel, rcv, tmp
        self.right, self.left = right, left

    def start_far(self):
        send, piece = self.copies.send, self.piece
        self.c1 = send(piece(2, 0), self.rel.at[0], self.right)
        self.c2 = send(piece(2, 1), self.rel.at[1], self.left)

    def start_near(self):
        send, piece = self.copies.send, self.piece
        self.c3 = send(piece(1, 1), self.rcv.at[0, 1], self.right)
        self.c4 = send(piece(3, 0), self.rcv.at[1, 0], self.left)

    def relay(self):
        send, piece = self.copies.send, self.piece
        self.c1.wait_recv()
        self.tmp[0] = (piece(1, 0)[...].astype(F32) + self.rel[0].astype(F32)).astype(BF16)
        self.c2.wait_recv()
        self.tmp[1] = (piece(3, 1)[...].astype(F32) + self.rel[1].astype(F32)).astype(BF16)
        self.c5 = send(self.tmp.at[0], self.rcv.at[0, 0], self.right)
        self.c6 = send(self.tmp.at[1], self.rcv.at[1, 1], self.left)

    def finish(self):
        for copy in (self.c3, self.c4, self.c5, self.c6):
            copy.wait_recv()
        return [
            self.piece(0, half)[...].astype(F32)
            + self.rcv[0, half].astype(F32)
            + self.rcv[1, half].astype(F32)
            for half in range(2)
        ]


class RingGather:
    def __init__(self, copies, block, right, left):
        self.copies, self.block, self.right, self.left = copies, block, right, left

    def start(self):
        whole = self.block(0, None)
        self.d1 = self.copies.send(whole, whole, self.right)
        self.d2 = self.copies.send(whole, whole, self.left)

    def relay(self):
        self.d1.wait_recv()
        far = self.block(3, 0)
        self.e1 = self.copies.send(far, far, self.right)
        self.d2.wait_recv()
        far = self.block(1, 1)
        self.e2 = self.copies.send(far, far, self.left)

    def finish(self):
        self.e1.wait_recv()
        self.e2.wait_recv()


def kernel(
    x_hbm, g_hbm, wq_hbm, wk_hbm, wv_hbm, wo_hbm,
    gin_ref, gq_ref, gk_ref, gv_ref, go_ref,
    xv, gv, wo, wfull, wt, proj, part,
    rel1, rcv1, tmp1, sum1, own1, rcv2, sum2, own2, rcv3,
    pd, att, grad, gall,
    wacc, wpart, wrcv1, wsum1, wrcv2, wrcv3, wfin,
    load_sem, send_sem, recv_sem,
):
    y, zh, x, zl, co = (lax.axis_index(n) for n in AXES)
    a = x * (1 - co) + y * co
    b = y * (1 - co) + x * co
    head = zl * 2 + co

    def dev(da=0, db=0, dc=0, dzl=0, dco=0):
        return (
            lax.rem(y + da * co + db * (1 - co), 4),
            lax.rem(zh + dc, 4),
            lax.rem(x + da * (1 - co) + db * co, 4),
            lax.rem(zl + dzl, 2),
            lax.rem(co + dco, 2),
        )

    a_to = [None] + [dev(da=k) for k in (1, 2, 3)]
    b_to = [None] + [dev(db=k) for k in (1, 2, 3)]
    z_to = [None] + [dev(dc=k) for k in (1, 2, 3)]
    h_core, h_chip, h_both = dev(dco=1), dev(dzl=1), dev(dzl=1, dco=1)
    near_first = (1, 3, 2)

    def rows_of(start, size):
        return pl.ds(pl.multiple_of(start, size), size)

    def place(at, off):
        return lax.rem(at + off, 4)

    mine = rows_of(head * WIDTH, WIDTH)
    load = lambda src, dst, k: pltpu.make_async_copy(src, dst, load_sem.at[k])
    load_w = [load(w.at[...], wfull.at[t, :, mine], t) for t, w in enumerate((wq_hbm, wk_hbm, wv_hbm))]
    load_x = [load(x_hbm.at[r], xv.at[r], 3 + r) for r in range(ROWS)]
    load_g = [load(g_hbm.at[r], gv.at[r], 7 + r) for r in range(ROWS)]
    load_o = load(wo_hbm, wo, 11)
    for copy in (load_w[0], load_w[1], *load_x):
        copy.start()

    barrier = pltpu.get_barrier_semaphore()
    friends = [*a_to[1:], *b_to[1:], *z_to[1:], h_core, h_chip, h_both]
    for friend in friends:
        pl.semaphore_signal(barrier, inc=1, device_id=friend, device_id_type=pl.DeviceIdType.MESH)

    copies = Copies(send_sem, recv_sem)
    def turn(t):
        load_w[t].wait()
        wt[t * WIDTH : (t + 1) * WIDTH, :] = wfull[t, :, mine].T

    def keep_projection(res, t, r):
        at = rows_of(r * HEAD_DIM, HEAD_DIM)
        for h in range(HEADS):
            proj[t, h, at, :] = res[h * HEAD_DIM : (h + 1) * HEAD_DIM].astype(BF16)

    turn(0)
    turn(1)
    for r in range(ROWS):
        load_x[r].wait()
        res = nt(wt[: 2 * WIDTH, :], xv[r])
        keep_projection(res[:WIDTH], 0, r)
        keep_projection(res[WIDTH:], 1, r)
    for copy in (load_w[2], load_o, *load_g):
        copy.start()

    def products(m, left, right, off):
        at = rows_of(place(a, off) * 128, 128)

        def one(h, _):
            part[m, h, at, :] = tn(proj[left, h, :, at], proj[right, h]).astype(BF16)
            return 0

        lax.fori_loop(0, HEADS, one, 0)

    order = (2, 1, 3, 0)

    def ring1(m, k):
        def piece(off, half):
            return part.at[m, half, rows_of(place(a, off) * 128 + place(b, k) * 32, 32), :]

        return RingSum(copies, piece, rel1.at[m, k], rcv1.at[m, k], tmp1.at[m, k], a_to[1], a_to[3])

    first = [[ring1(m, k) for k in range(4)] for m in range(2)]

    def start_first(m, left, right):
        products(m, left, right, 2)
        products(m, left, right, 1)
        if m == 0:
            pl.semaphore_wait(barrier, len(friends))
        for k in order:
            first[m][k].start_far()
        products(m, left, right, 3)
        products(m, left, right, 0)
        for k in order:
            first[m][k].start_near()

    start_first(0, 0, 1)
    turn(2)
    load_o.wait()
    for copy in load_g:
        copy.wait()

    def project_rest(r, _):
        keep_projection(nt(wt[2 * WIDTH :, :], xv[r]), 2, r)
        keep_projection(nt(wo[...], gv[r]), 3, r)
        return 0

    lax.fori_loop(0, ROWS, project_rest, 0)
    for k in order:
        first[0][k].relay()
    start_first(1, 3, 2)

    second = [[None] * 4 for _ in range(2)]

    def end_first(m):
        for k in order:
            for half, total in enumerate(first[m][k].finish()):
                if k:
                    sum1[m, k - 1, half] = total.astype(BF16)
                else:
                    own1[m, half] = total
            if k:
                second[m][k] = copies.send(sum1.at[m, k - 1], rcv2.at[m, k - 1], b_to[k])

    def spot(off):
        at = place(zh, off)
        return at // 2, rows_of(lax.rem(at, 2) * 16, 16)

    third = [[None] * 4 for _ in range(2)]

    def end_second(m):
        total = own1[m]
        for k in near_first:
            second[m][k].wait_recv()
            total = total + rcv2[m, k - 1].astype(F32)
        sum2[m] = total.astype(BF16)
        own2[m] = total
        for k in (2, 1, 3):
            h, at = spot(k)
            third[m][k] = copies.send(sum2.at[m, h, at, :], rcv3.at[m, k - 1], z_to[k])

    end_first(0)
    for k in order:
        first[1][k].relay()
    end_second(0)
    end_first(1)

    end_second(1)

    def end_third(m):
        h, at = spot(0)
        total = own2[m, h, at, :]
        for k in near_first:
            third[m][k].wait_recv()
            total = total + rcv3[m, k - 1].astype(F32)
        return total

    exponent = jnp.exp(C * end_third(0))
    probs = exponent / jnp.sum(exponent, axis=1, keepdims=True)
    own_h, _ = spot(0)
    own_rows = rows_of(a * 128 + b * 32 + lax.rem(zh, 2) * 16, 16)
    pd[0, own_h, own_rows, :] = probs.astype(BF16)
    grad_probs = end_third(1)
    inner = jnp.sum(probs * grad_probs, axis=1, keepdims=True)
    pd[1, own_h, own_rows, :] = (C * probs * (grad_probs - inner)).astype(BF16)
    spread = [[], []]
    for m in range(2):
        own = pd.at[m, own_h, own_rows, :]
        spread[m] = [copies.send(own, own, z_to[k]) for k in (2, 1, 3)]

    def block(m, k):
        def at(off, half):
            rows = rows_of(place(a, off) * 128 + place(b, k) * 32, 32)
            return pd.at[m, :, rows, :] if half is None else pd.at[m, half, rows, :]

        return at

    gather_a = [
        [RingGather(copies, block(m, k), a_to[1], a_to[3]) for k in range(4)] for m in range(2)
    ]
    gather_b = [[None] * 4 for _ in range(2)]
    for m in range(2):
        for copy in spread[m]:
            copy.wait_recv()
        own = block(m, 0)(0, None)
        for k in (2, 1, 3):
            gather_b[m][k] = copies.send(own, own, b_to[k])
        gather_a[m][0].start()

    to_core = [copies.send(wfull.at[t, :, mine], wfull.at[t, :, mine], h_core) for t in range(3)]
    to_chip = [copies.send(wfull.at[t, :, mine], wfull.at[t, :, mine], h_chip) for t in range(3)]

    def pass_on(m, k):
        gather_b[m][(4 - k) % 4].wait_recv()
        gather_a[m][k].start()

    gather_a[0][0].relay()
    for m in range(2):
        for k in near_first:
            pass_on(m, k)
        if m == 0:
            gather_a[1][0].relay()
    for m, k in ((0, 1), (0, 3), (0, 2), (1, 1), (1, 3)):
        gather_a[m][k].relay()

    def pair_value(h, _):
        p = pd[0, h]
        att[h] = nt(proj[2, h], p).astype(BF16).reshape(ROWS, HEAD_DIM, COLS)
        grad[2, h] = nn(proj[3, h], p).astype(BF16).reshape(ROWS, HEAD_DIM, COLS)
        return 0

    def pair_score(h, _):
        d = pd[1, h]
        grad[0, h] = nt(proj[1, h], d).astype(BF16).reshape(ROWS, HEAD_DIM, COLS)
        grad[1, h] = nn(proj[0, h], d).astype(BF16).reshape(ROWS, HEAD_DIM, COLS)
        return 0

    def to_heads(t):
        sent = []
        for device, dzl, dco in ((h_chip, 1, 0), (h_both, 1, 1), (h_core, 0, 1)):
            at = rows_of((lax.rem(zl + dzl, 2) * 2 + lax.rem(co + dco, 2)) * 128, 128)
            sent.append(copies.send(grad.at[t, :, :, :, at], gall.at[t, head], device))
        keep = pltpu.make_async_copy(grad.at[t, :, :, :, mine], gall.at[t, head], load_sem.at[12 + t])
        keep.start()
        return sent, keep

    def weight_part(p, kinds):
        def one(r, _):
            for k, (source, t) in enumerate(kinds):
                src = att if t is None else grad.at[t]
                lhs = jnp.concatenate([src[0, r], src[1, r]], axis=0)
                at = slice(k * WIDTH, (k + 1) * WIDTH)
                wacc[at, :] = jnp.where(r == 0, 0.0, wacc[at, :]) + nn(lhs, source[r])
            return 0

        lax.fori_loop(0, ROWS, one, 0)
        wpart[p] = wacc[...].astype(BF16)

    wfirst = [[None] * 4 for _ in range(2)]
    wsecond = [[None] * 4 for _ in range(2)]
    wthird = [[None] * 4 for _ in range(2)]

    def start_weights(p):
        for k in (2, 1, 3):
            wfirst[p][k] = copies.send(
                wpart.at[p, rows_of(place(a, k) * 64, 64), :], wrcv1.at[p, k - 1], a_to[k]
            )

    def end_wfirst(p):
        total = wpart[p, rows_of(a * 64, 64), :].astype(F32)
        for k in near_first:
            wfirst[p][k].wait_recv()
            total = total + wrcv1[p, k - 1].astype(F32)
        wsum1[p] = total.astype(BF16)
        for k in (2, 1, 3):
            wsecond[p][k] = copies.send(
                wsum1.at[p, rows_of(place(b, k) * 16, 16), :], wrcv2.at[p, k - 1], b_to[k]
            )

    def end_wsecond(p):
        total = wsum1[p, rows_of(b * 16, 16), :].astype(F32)
        for k in near_first:
            wsecond[p][k].wait_recv()
            total = total + wrcv2[p, k - 1].astype(F32)
        wrcv3[p, zh] = total.astype(BF16)
        own = wrcv3.at[p, zh]
        for k in (2, 1, 3):
            wthird[p][k] = copies.send(own, own, z_to[k])

    wgather_b = [[None] * 4 for _ in range(2)]
    wgather_a = [[], []]

    def wblock(p, k):
        return wfin.at[p, rows_of(a * 64 + place(b, k) * 16, 16), :]

    def spread_weights(p, k):
        own = wblock(p, k)
        for d in (2, 1, 3):
            wgather_a[p].append(copies.send(own, own, a_to[d]))

    def end_wthird(p):
        for k in near_first:
            wthird[p][k].wait_recv()
        total = wrcv3[p, 0].astype(F32) + wrcv3[p, 1].astype(F32)
        total = total + wrcv3[p, 2].astype(F32) + wrcv3[p, 3].astype(F32)
        wfin[p, rows_of(a * 64 + b * 16, 16), :] = total.astype(BF16)
        own = wblock(p, 0)
        for k in (2, 1, 3):
            wgather_b[p][k] = copies.send(own, own, b_to[k])
        spread_weights(p, 0)

    def pass_on_weights(p):
        for k in near_first:
            wgather_b[p][(4 - k) % 4].wait_recv()
            spread_weights(p, k)

    for k in range(4):
        gather_a[0][k].finish()
    lax.fori_loop(0, HEADS, pair_value, 0)
    gather_a[1][2].relay()
    theirs = rows_of((lax.rem(zl + 1, 2) * 2 + co) * WIDTH, WIDTH)
    forward = []
    for t in range(3):
        to_chip[t].wait_recv()
        forward.append(copies.send(wfull.at[t, :, theirs], wfull.at[t, :, theirs], h_core))
    moved = {2: to_heads(2)}
    weight_part(0, ((xv, 2), (gv, None)))
    start_weights(0)
    for k in range(4):
        gather_a[1][k].finish()
    lax.fori_loop(0, HEADS, pair_score, 0)
    moved[0] = to_heads(0)
    moved[1] = to_heads(1)
    weight_part(1, ((xv, 0), (xv, 1)))
    start_weights(1)
    end_wfirst(0)
    end_wsecond(0)
    end_wfirst(1)
    end_wsecond(1)
    end_wthird(0)
    pass_on_weights(0)
    end_wthird(1)

    for copy in to_core + forward:
        copy.wait_recv()
    for t in range(3):
        sent, keep = moved[t]
        keep.wait()
        for copy in sent:
            copy.wait_recv()
    pass_on_weights(1)

    def block_inputs(k, _):
        r = k * 2
        total = None
        for t in range(3):
            sides = [
                jnp.concatenate([gall[t, hd, h, r + s] for hd in range(4) for h in range(HEADS)], axis=0)
                for s in range(2)
            ]
            term = nn(wfull[t], jnp.concatenate(sides, axis=1))
            total = term if total is None else total + term
        flat = total.T.astype(BF16)
        gin_ref[r] = flat[:128]
        gin_ref[r + 1] = flat[128:]
        return 0

    lax.fori_loop(0, 2, block_inputs, 0)
    for p in range(2):
        for copy in wgather_a[p]:
            copy.wait_recv()
    gv_ref[...] = wfin[0, :WIDTH].T
    go_ref[...] = wfin[0, WIDTH:]
    gq_ref[...] = wfin[1, :WIDTH].T
    gk_ref[...] = wfin[1, WIDTH:].T
    copies.drain()


def last_step(*refs):
    sources, outs, held, made, sem = refs[:5], refs[5:10], refs[10:15], refs[15:19], refs[19]
    into = [pltpu.make_async_copy(sources[k], held[k], sem.at[k]) for k in range(5)]
    back = [pltpu.make_async_copy(held[0] if k == 0 else made[k - 1], outs[k], sem.at[5 + k]) for k in range(5)]
    for copy in into:
        copy.start()
    for k in range(5):
        into[k].wait()
        if k:
            made[k - 1][...] = held[k][...].astype(F32) * INV_ROOT
        back[k].start()
    for copy in back:
        copy.wait()


def body(inputs, out_grad, w_query, w_key, w_value, w_output):
    vmem = lambda *shape: pltpu.VMEM(shape, BF16)
    gin, gq, gk, gv, go = pl.pallas_call(
        kernel,
        out_shape=(
            jax.ShapeDtypeStruct((ROWS, 128, D), BF16),
            *(jax.ShapeDtypeStruct((D, WIDTH), BF16) for _ in range(3)),
            jax.ShapeDtypeStruct((WIDTH, D), BF16),
        ),
        in_specs=[pl.BlockSpec(memory_space=pltpu.HBM)] * 6,
        out_specs=(pl.BlockSpec(memory_space=pltpu.VMEM),) * 5,
        scratch_shapes=[
            vmem(ROWS, COLS, D),
            vmem(ROWS, COLS, D),
            vmem(WIDTH, D),
            vmem(3, D, 4 * WIDTH),
            vmem(3 * WIDTH, D),
            vmem(4, HEADS, ROWS * HEAD_DIM, COLS),
            vmem(2, HEADS, COLS, COLS),
            vmem(2, 4, 2, 32, COLS),
            vmem(2, 4, 2, 2, 32, COLS),
            vmem(2, 4, 2, 32, COLS),
            vmem(2, 3, HEADS, 32, COLS),
            pltpu.VMEM((2, HEADS, 32, COLS), F32),
            vmem(2, 3, HEADS, 32, COLS),
            vmem(2, HEADS, 32, COLS),
            pltpu.VMEM((2, HEADS, 32, COLS), F32),
            vmem(2, 3, 16, COLS),
            vmem(2, HEADS, COLS, COLS),
            vmem(HEADS, ROWS, HEAD_DIM, COLS),
            vmem(3, HEADS, ROWS, HEAD_DIM, COLS),
            vmem(3, 4, HEADS, ROWS, HEAD_DIM, 128),
            pltpu.VMEM((2 * WIDTH, D), F32),
            vmem(2, 2 * WIDTH, D),
            vmem(2, 3, 64, D),
            vmem(2, 64, D),
            vmem(2, 3, 16, D),
            vmem(2, 4, 16, D),
            vmem(2, 2 * WIDTH, D),
            pltpu.SemaphoreType.DMA((15,)),
            pltpu.SemaphoreType.DMA((COPIES,)),
            pltpu.SemaphoreType.DMA((COPIES,)),
        ],
        compiler_params=pltpu.CompilerParams(
            collective_id=0, has_side_effects=True, vmem_limit_bytes=56 * 1024 * 1024
        ),
        name="tied_row_attention_grad",
    )(inputs, out_grad, w_query, w_key, w_value, w_output)
    return pl.pallas_call(
        last_step,
        out_shape=(
            jax.ShapeDtypeStruct((ROWS, 128, D), BF16),
            *(jax.ShapeDtypeStruct((D, WIDTH), F32) for _ in range(3)),
            jax.ShapeDtypeStruct((WIDTH, D), F32),
        ),
        in_specs=[pl.BlockSpec(memory_space=pl.ANY)] * 5,
        out_specs=(pl.BlockSpec(memory_space=pl.ANY),) * 5,
        scratch_shapes=[
            vmem(ROWS, 128, D),
            *(vmem(D, WIDTH) for _ in range(3)),
            vmem(WIDTH, D),
            *(pltpu.VMEM((D, WIDTH), F32) for _ in range(3)),
            pltpu.VMEM((WIDTH, D), F32),
            pltpu.SemaphoreType.DMA((10,)),
        ],
        compiler_params=pltpu.CompilerParams(vmem_limit_bytes=60 * 1024 * 1024),
        name="scale_weight_grads",
    )(gin, gq, gk, gv, go)


def solution(mesh):
    finer = Mesh(mesh.devices.reshape(4, 4, 4, 2, 2), AXES)
    return jax.shard_map(
        body,
        mesh=finer,
        in_specs=(
            P(SEQ, None, None),
            P(SEQ, None, None),
            P(None, HEAD),
            P(None, HEAD),
            P(None, HEAD),
            P(HEAD, None),
        ),
        out_specs=(
            P(SEQ, HEAD, None),
            P(None, HEAD),
            P(None, HEAD),
            P(None, HEAD),
            P(HEAD, None),
        ),
        check_vma=False,
    )
```

```python
import math

import jax
import jax.numpy as jnp
from jax import lax
from jax.experimental import pallas as pl
from jax.experimental.pallas import tpu as pltpu
from jax.sharding import Mesh
from jax.sharding import PartitionSpec as P

AXES = ("y", "zh", "x", "zl", "core")
SEQ = ("y", "zh", "x")
HEAD = ("zl", "core")
ROWS, COLS, D, HEAD_DIM, HEADS = 4, 512, 768, 64, 2
WIDTH = HEADS * HEAD_DIM
ALL_ROWS = 256
C = 1.0 / (math.sqrt(HEAD_DIM) * math.sqrt(ALL_ROWS))
INV_ROOT = 1.0 / math.sqrt(ALL_ROWS * COLS)
COPIES = 176
F32, BF16 = jnp.float32, jnp.bfloat16


def nt(a, b):
    return lax.dot_general(a, b, (((1,), (1,)), ((), ())), preferred_element_type=F32)


def nn(a, b):
    return lax.dot_general(a, b, (((1,), (0,)), ((), ())), preferred_element_type=F32)


def tn(a, b):
    return lax.dot_general(a, b, (((0,), (0,)), ((), ())), preferred_element_type=F32)


class Copies:
    def __init__(self, send_sem, recv_sem):
        self.send_sem, self.recv_sem, self.made = send_sem, recv_sem, []

    def send(self, src, dst, device):
        k = len(self.made)
        copy = pltpu.make_async_remote_copy(
            src_ref=src,
            dst_ref=dst,
            send_sem=self.send_sem.at[k],
            recv_sem=self.recv_sem.at[k],
            device_id=device,
            device_id_type=pl.DeviceIdType.MESH,
        )
        copy.start()
        self.made.append(copy)
        return copy

    def drain(self):
        for copy in self.made:
            copy.wait_send()


class RingSum:
    def __init__(self, copies, piece, rel, rcv, tmp, right, left):
        self.copies, self.piece, self.rel, self.rcv, self.tmp = copies, piece, rel, rcv, tmp
        self.right, self.left = right, left

    def start_far(self):
        send, piece = self.copies.send, self.piece
        self.c1 = send(piece(2, 0), self.rel.at[0], self.right)
        self.c2 = send(piece(2, 1), self.rel.at[1], self.left)

    def start_near(self):
        send, piece = self.copies.send, self.piece
        self.c3 = send(piece(1, 1), self.rcv.at[0, 1], self.right)
        self.c4 = send(piece(3, 0), self.rcv.at[1, 0], self.left)

    def relay(self):
        send, piece = self.copies.send, self.piece
        self.c1.wait_recv()
        self.tmp[0] = (piece(1, 0)[...].astype(F32) + self.rel[0].astype(F32)).astype(BF16)
        self.c2.wait_recv()
        self.tmp[1] = (piece(3, 1)[...].astype(F32) + self.rel[1].astype(F32)).astype(BF16)
        self.c5 = send(self.tmp.at[0], self.rcv.at[0, 0], self.right)
        self.c6 = send(self.tmp.at[1], self.rcv.at[1, 1], self.left)

    def finish(self):
        for copy in (self.c3, self.c4, self.c5, self.c6):
            copy.wait_recv()
        return [
            self.piece(0, half)[...].astype(F32)
            + self.rcv[0, half].astype(F32)
            + self.rcv[1, half].astype(F32)
            for half in range(2)
        ]


class RingGather:
    def __init__(self, copies, block, right, left):
        self.copies, self.block, self.right, self.left = copies, block, right, left

    def start(self):
        whole = self.block(0, None)
        self.d1 = self.copies.send(whole, whole, self.right)
        self.d2 = self.copies.send(whole, whole, self.left)

    def relay(self):
        self.d1.wait_recv()
        far = self.block(3, 0)
        self.e1 = self.copies.send(far, far, self.right)
        self.d2.wait_recv()
        far = self.block(1, 1)
        self.e2 = self.copies.send(far, far, self.left)

    def finish(self):
        self.e1.wait_recv()
        self.e2.wait_recv()


def kernel(
    x_hbm, g_hbm, wq_hbm, wk_hbm, wv_hbm, wo_hbm,
    gin_ref, gq_ref, gk_ref, gv_ref, go_ref,
    xv, gv, wo, wfull, wt, proj, part,
    rel1, rcv1, tmp1, sum1, own1, rcv2, sum2, own2, rcv3,
    pd, att, grad, gall,
    wacc, wpart, wrcv1, wsum1, wrcv2, wrcv3, wfin,
    load_sem, send_sem, recv_sem,
):
    y, zh, x, zl, co = (lax.axis_index(n) for n in AXES)
    a = x * (1 - co) + y * co
    b = y * (1 - co) + x * co
    head = zl * 2 + co

    def dev(da=0, db=0, dc=0, dzl=0, dco=0):
        return (
            lax.rem(y + da * co + db * (1 - co), 4),
            lax.rem(zh + dc, 4),
            lax.rem(x + da * (1 - co) + db * co, 4),
            lax.rem(zl + dzl, 2),
            lax.rem(co + dco, 2),
        )

    a_to = [None] + [dev(da=k) for k in (1, 2, 3)]
    b_to = [None] + [dev(db=k) for k in (1, 2, 3)]
    z_to = [None] + [dev(dc=k) for k in (1, 2, 3)]
    h_core, h_chip, h_both = dev(dco=1), dev(dzl=1), dev(dzl=1, dco=1)
    near_first = (1, 3, 2)

    def rows_of(start, size):
        return pl.ds(pl.multiple_of(start, size), size)

    def place(at, off):
        return lax.rem(at + off, 4)

    mine = rows_of(head * WIDTH, WIDTH)
    load = lambda src, dst, k: pltpu.make_async_copy(src, dst, load_sem.at[k])
    load_w = [load(w.at[...], wfull.at[t, :, mine], t) for t, w in enumerate((wq_hbm, wk_hbm, wv_hbm))]
    load_x = [load(x_hbm.at[r], xv.at[r], 3 + r) for r in range(ROWS)]
    load_g = [load(g_hbm.at[r], gv.at[r], 7 + r) for r in range(ROWS)]
    load_o = load(wo_hbm, wo, 11)
    for copy in (load_w[0], load_w[1], *load_x):
        copy.start()

    barrier = pltpu.get_barrier_semaphore()
    friends = [*a_to[1:], *b_to[1:], *z_to[1:], h_core, h_chip, h_both]
    for friend in friends:
        pl.semaphore_signal(barrier, inc=1, device_id=friend, device_id_type=pl.DeviceIdType.MESH)

    copies = Copies(send_sem, recv_sem)
    def turn(t):
        load_w[t].wait()
        wt[t * WIDTH : (t + 1) * WIDTH, :] = wfull[t, :, mine].T

    def keep_projection(res, t, r):
        at = rows_of(r * HEAD_DIM, HEAD_DIM)
        for h in range(HEADS):
            proj[t, h, at, :] = res[h * HEAD_DIM : (h + 1) * HEAD_DIM].astype(BF16)

    turn(0)
    turn(1)
    for r in range(ROWS):
        load_x[r].wait()
        res = nt(wt[: 2 * WIDTH, :], xv[r])
        keep_projection(res[:WIDTH], 0, r)
        keep_projection(res[WIDTH:], 1, r)
    for copy in (load_w[2], load_o, *load_g):
        copy.start()

    def products(m, left, right, off):
        at = rows_of(place(a, off) * 128, 128)

        def one(h, _):
            part[m, h, at, :] = tn(proj[left, h, :, at], proj[right, h]).astype(BF16)
            return 0

        lax.fori_loop(0, HEADS, one, 0)

    order = (2, 1, 3, 0)

    def ring1(m, k):
        def piece(off, half):
            return part.at[m, half, rows_of(place(a, off) * 128 + place(b, k) * 32, 32), :]

        return RingSum(copies, piece, rel1.at[m, k], rcv1.at[m, k], tmp1.at[m, k], a_to[1], a_to[3])

    first = [[ring1(m, k) for k in range(4)] for m in range(2)]

    def start_first(m, left, right):
        products(m, left, right, 2)
        products(m, left, right, 1)
        if m == 0:
            pl.semaphore_wait(barrier, len(friends))
        for k in order:
            first[m][k].start_far()
        products(m, left, right, 3)
        products(m, left, right, 0)
        for k in order:
            first[m][k].start_near()

    start_first(0, 0, 1)
    turn(2)
    load_o.wait()
    for copy in load_g:
        copy.wait()

    def project_rest(r, _):
        keep_projection(nt(wt[2 * WIDTH :, :], xv[r]), 2, r)
        keep_projection(nt(wo[...], gv[r]), 3, r)
        return 0

    lax.fori_loop(0, ROWS, project_rest, 0)
    for k in order:
        first[0][k].relay()
    start_first(1, 3, 2)

    second = [[None] * 4 for _ in range(2)]

    def end_first(m):
        for k in order:
            for half, total in enumerate(first[m][k].finish()):
                if k:
                    sum1[m, k - 1, half] = total.astype(BF16)
                else:
                    own1[m, half] = total
            if k:
                second[m][k] = copies.send(sum1.at[m, k - 1], rcv2.at[m, k - 1], b_to[k])

    def spot(off):
        at = place(zh, off)
        return at // 2, rows_of(lax.rem(at, 2) * 16, 16)

    third = [[None] * 4 for _ in range(2)]

    def end_second(m):
        total = own1[m]
        for k in near_first:
            second[m][k].wait_recv()
            total = total + rcv2[m, k - 1].astype(F32)
        sum2[m] = total.astype(BF16)
        own2[m] = total
        for k in (2, 1, 3):
            h, at = spot(k)
            third[m][k] = copies.send(sum2.at[m, h, at, :], rcv3.at[m, k - 1], z_to[k])

    end_first(0)
    for k in order:
        first[1][k].relay()
    end_second(0)
    end_first(1)

    end_second(1)

    def end_third(m):
        h, at = spot(0)
        total = own2[m, h, at, :]
        for k in near_first:
            third[m][k].wait_recv()
            total = total + rcv3[m, k - 1].astype(F32)
        return total

    exponent = jnp.exp(C * end_third(0))
    probs = exponent / jnp.sum(exponent, axis=1, keepdims=True)
    own_h, _ = spot(0)
    own_rows = rows_of(a * 128 + b * 32 + lax.rem(zh, 2) * 16, 16)
    pd[0, own_h, own_rows, :] = probs.astype(BF16)

    def to_third(m):
        own = pd.at[m, own_h, own_rows, :]
        return [copies.send(own, own, z_to[k]) for k in (2, 1, 3)]

    spread = [to_third(0)]
    grad_probs = end_third(1)
    inner = jnp.sum(probs * grad_probs, axis=1, keepdims=True)
    pd[1, own_h, own_rows, :] = (C * probs * (grad_probs - inner)).astype(BF16)
    spread.append(to_third(1))

    def block(m, k):
        def at(off, half):
            rows = rows_of(place(a, off) * 128 + place(b, k) * 32, 32)
            return pd.at[m, :, rows, :] if half is None else pd.at[m, half, rows, :]

        return at

    gather_a = [
        [RingGather(copies, block(m, k), a_to[1], a_to[3]) for k in range(4)] for m in range(2)
    ]
    gather_b = [[None] * 4 for _ in range(2)]
    for m in range(2):
        for copy in spread[m]:
            copy.wait_recv()
        own = block(m, 0)(0, None)
        for k in (2, 1, 3):
            gather_b[m][k] = copies.send(own, own, b_to[k])
        gather_a[m][0].start()

    to_core = [copies.send(wfull.at[t, :, mine], wfull.at[t, :, mine], h_core) for t in range(3)]
    to_chip = [copies.send(wfull.at[t, :, mine], wfull.at[t, :, mine], h_chip) for t in range(3)]

    def pass_on(m, k):
        gather_b[m][(4 - k) % 4].wait_recv()
        gather_a[m][k].start()

    gather_a[0][0].relay()
    for m in range(2):
        for k in near_first:
            pass_on(m, k)
        if m == 0:
            gather_a[1][0].relay()
    for m, k in ((0, 1), (0, 3), (0, 2), (1, 1), (1, 3)):
        gather_a[m][k].relay()

    def pair_value(h, _):
        p = pd[0, h]
        att[h] = nt(proj[2, h], p).astype(BF16).reshape(ROWS, HEAD_DIM, COLS)
        grad[2, h] = nn(proj[3, h], p).astype(BF16).reshape(ROWS, HEAD_DIM, COLS)
        return 0

    def pair_score(h, _):
        d = pd[1, h]
        grad[0, h] = nt(proj[1, h], d).astype(BF16).reshape(ROWS, HEAD_DIM, COLS)
        grad[1, h] = nn(proj[0, h], d).astype(BF16).reshape(ROWS, HEAD_DIM, COLS)
        return 0

    def to_heads(t):
        sent = []
        for device, dzl, dco in ((h_chip, 1, 0), (h_both, 1, 1), (h_core, 0, 1)):
            at = rows_of((lax.rem(zl + dzl, 2) * 2 + lax.rem(co + dco, 2)) * 128, 128)
            sent.append(copies.send(grad.at[t, :, :, :, at], gall.at[t, head], device))
        keep = pltpu.make_async_copy(grad.at[t, :, :, :, mine], gall.at[t, head], load_sem.at[12 + t])
        keep.start()
        return sent, keep

    def weight_part(p, kinds):
        def one(r, _):
            for k, (source, t) in enumerate(kinds):
                src = att if t is None else grad.at[t]
                lhs = jnp.concatenate([src[0, r], src[1, r]], axis=0)
                at = slice(k * WIDTH, (k + 1) * WIDTH)
                wacc[at, :] = jnp.where(r == 0, 0.0, wacc[at, :]) + nn(lhs, source[r])
            return 0

        lax.fori_loop(0, ROWS, one, 0)
        wpart[p] = wacc[...].astype(BF16)

    wfirst = [[None] * 4 for _ in range(2)]
    wsecond = [[None] * 4 for _ in range(2)]
    wthird = [[None] * 4 for _ in range(2)]

    def start_weights(p):
        for k in (2, 1, 3):
            wfirst[p][k] = copies.send(
                wpart.at[p, rows_of(place(a, k) * 64, 64), :], wrcv1.at[p, k - 1], a_to[k]
            )

    def end_wfirst(p):
        total = wpart[p, rows_of(a * 64, 64), :].astype(F32)
        for k in near_first:
            wfirst[p][k].wait_recv()
            total = total + wrcv1[p, k - 1].astype(F32)
        wsum1[p] = total.astype(BF16)
        for k in (2, 1, 3):
            wsecond[p][k] = copies.send(
                wsum1.at[p, rows_of(place(b, k) * 16, 16), :], wrcv2.at[p, k - 1], b_to[k]
            )

    def end_wsecond(p):
        total = wsum1[p, rows_of(b * 16, 16), :].astype(F32)
        for k in near_first:
            wsecond[p][k].wait_recv()
            total = total + wrcv2[p, k - 1].astype(F32)
        wrcv3[p, zh] = total.astype(BF16)
        own = wrcv3.at[p, zh]
        for k in (2, 1, 3):
            wthird[p][k] = copies.send(own, own, z_to[k])

    wgather_b = [[None] * 4 for _ in range(2)]
    wgather_a = [[], []]

    def wblock(p, k):
        return wfin.at[p, rows_of(a * 64 + place(b, k) * 16, 16), :]

    def spread_weights(p, k):
        own = wblock(p, k)
        for d in (2, 1, 3):
            wgather_a[p].append(copies.send(own, own, a_to[d]))

    def end_wthird(p):
        for k in near_first:
            wthird[p][k].wait_recv()
        total = wrcv3[p, 0].astype(F32) + wrcv3[p, 1].astype(F32)
        total = total + wrcv3[p, 2].astype(F32) + wrcv3[p, 3].astype(F32)
        wfin[p, rows_of(a * 64 + b * 16, 16), :] = total.astype(BF16)
        own = wblock(p, 0)
        for k in (2, 1, 3):
            wgather_b[p][k] = copies.send(own, own, b_to[k])
        spread_weights(p, 0)

    def pass_on_weights(p):
        for k in near_first:
            wgather_b[p][(4 - k) % 4].wait_recv()
            spread_weights(p, k)

    for k in range(4):
        gather_a[0][k].finish()
    lax.fori_loop(0, HEADS, pair_value, 0)
    gather_a[1][2].relay()
    theirs = rows_of((lax.rem(zl + 1, 2) * 2 + co) * WIDTH, WIDTH)
    forward = []
    for t in range(3):
        to_chip[t].wait_recv()
        forward.append(copies.send(wfull.at[t, :, theirs], wfull.at[t, :, theirs], h_core))
    moved = {2: to_heads(2)}
    weight_part(0, ((xv, 2), (gv, None)))
    start_weights(0)
    for k in range(4):
        gather_a[1][k].finish()
    lax.fori_loop(0, HEADS, pair_score, 0)
    moved[0] = to_heads(0)
    moved[1] = to_heads(1)
    weight_part(1, ((xv, 0), (xv, 1)))
    start_weights(1)
    end_wfirst(0)
    end_wsecond(0)
    end_wfirst(1)
    end_wsecond(1)
    end_wthird(0)
    pass_on_weights(0)
    end_wthird(1)

    for copy in to_core + forward:
        copy.wait_recv()
    for t in range(3):
        sent, keep = moved[t]
        keep.wait()
        for copy in sent:
            copy.wait_recv()
    pass_on_weights(1)

    def block_inputs(k, _):
        r = k * 2
        total = None
        for t in range(3):
            sides = [
                jnp.concatenate([gall[t, hd, h, r + s] for hd in range(4) for h in range(HEADS)], axis=0)
                for s in range(2)
            ]
            term = nn(wfull[t], jnp.concatenate(sides, axis=1))
            total = term if total is None else total + term
        flat = total.T.astype(BF16)
        gin_ref[r] = flat[:128]
        gin_ref[r + 1] = flat[128:]
        return 0

    lax.fori_loop(0, 2, block_inputs, 0)
    for p in range(2):
        for copy in wgather_a[p]:
            copy.wait_recv()
    gv_ref[...] = wfin[0, :WIDTH].T
    go_ref[...] = wfin[0, WIDTH:]
    gq_ref[...] = wfin[1, :WIDTH].T
    gk_ref[...] = wfin[1, WIDTH:].T
    copies.drain()


def last_step(*refs):
    sources, outs, held, made, sem = refs[:5], refs[5:10], refs[10:15], refs[15:19], refs[19]
    into = [pltpu.make_async_copy(sources[k], held[k], sem.at[k]) for k in range(5)]
    back = [pltpu.make_async_copy(held[0] if k == 0 else made[k - 1], outs[k], sem.at[5 + k]) for k in range(5)]
    for copy in into:
        copy.start()
    for k in range(5):
        into[k].wait()
        if k:
            made[k - 1][...] = held[k][...].astype(F32) * INV_ROOT
        back[k].start()
    for copy in back:
        copy.wait()


def body(inputs, out_grad, w_query, w_key, w_value, w_output):
    vmem = lambda *shape: pltpu.VMEM(shape, BF16)
    gin, gq, gk, gv, go = pl.pallas_call(
        kernel,
        out_shape=(
            jax.ShapeDtypeStruct((ROWS, 128, D), BF16),
            *(jax.ShapeDtypeStruct((D, WIDTH), BF16) for _ in range(3)),
            jax.ShapeDtypeStruct((WIDTH, D), BF16),
        ),
        in_specs=[pl.BlockSpec(memory_space=pltpu.HBM)] * 6,
        out_specs=(pl.BlockSpec(memory_space=pltpu.VMEM),) * 5,
        scratch_shapes=[
            vmem(ROWS, COLS, D),
            vmem(ROWS, COLS, D),
            vmem(WIDTH, D),
            vmem(3, D, 4 * WIDTH),
            vmem(3 * WIDTH, D),
            vmem(4, HEADS, ROWS * HEAD_DIM, COLS),
            vmem(2, HEADS, COLS, COLS),
            vmem(2, 4, 2, 32, COLS),
            vmem(2, 4, 2, 2, 32, COLS),
            vmem(2, 4, 2, 32, COLS),
            vmem(2, 3, HEADS, 32, COLS),
            pltpu.VMEM((2, HEADS, 32, COLS), F32),
            vmem(2, 3, HEADS, 32, COLS),
            vmem(2, HEADS, 32, COLS),
            pltpu.VMEM((2, HEADS, 32, COLS), F32),
            vmem(2, 3, 16, COLS),
            vmem(2, HEADS, COLS, COLS),
            vmem(HEADS, ROWS, HEAD_DIM, COLS),
            vmem(3, HEADS, ROWS, HEAD_DIM, COLS),
            vmem(3, 4, HEADS, ROWS, HEAD_DIM, 128),
            pltpu.VMEM((2 * WIDTH, D), F32),
            vmem(2, 2 * WIDTH, D),
            vmem(2, 3, 64, D),
            vmem(2, 64, D),
            vmem(2, 3, 16, D),
            vmem(2, 4, 16, D),
            vmem(2, 2 * WIDTH, D),
            pltpu.SemaphoreType.DMA((15,)),
            pltpu.SemaphoreType.DMA((COPIES,)),
            pltpu.SemaphoreType.DMA((COPIES,)),
        ],
        compiler_params=pltpu.CompilerParams(
            collective_id=0, has_side_effects=True, vmem_limit_bytes=56 * 1024 * 1024
        ),
        name="tied_row_attention_grad",
    )(inputs, out_grad, w_query, w_key, w_value, w_output)
    return pl.pallas_call(
        last_step,
        out_shape=(
            jax.ShapeDtypeStruct((ROWS, 128, D), BF16),
            *(jax.ShapeDtypeStruct((D, WIDTH), F32) for _ in range(3)),
            jax.ShapeDtypeStruct((WIDTH, D), F32),
        ),
        in_specs=[pl.BlockSpec(memory_space=pl.ANY)] * 5,
        out_specs=(pl.BlockSpec(memory_space=pl.ANY),) * 5,
        scratch_shapes=[
            vmem(ROWS, 128, D),
            *(vmem(D, WIDTH) for _ in range(3)),
            vmem(WIDTH, D),
            *(pltpu.VMEM((D, WIDTH), F32) for _ in range(3)),
            pltpu.VMEM((WIDTH, D), F32),
            pltpu.SemaphoreType.DMA((10,)),
        ],
        compiler_params=pltpu.CompilerParams(vmem_limit_bytes=60 * 1024 * 1024),
        name="scale_weight_grads",
    )(gin, gq, gk, gv, go)


def solution(mesh):
    finer = Mesh(mesh.devices.reshape(4, 4, 4, 2, 2), AXES)
    return jax.shard_map(
        body,
        mesh=finer,
        in_specs=(
            P(SEQ, None, None),
            P(SEQ, None, None),
            P(None, HEAD),
            P(None, HEAD),
            P(None, HEAD),
            P(HEAD, None),
        ),
        out_specs=(
            P(SEQ, HEAD, None),
            P(None, HEAD),
            P(None, HEAD),
            P(None, HEAD),
            P(HEAD, None),
        ),
        check_vma=False,
    )
```
